32 devices in a mesh: expert: 8 (over z, x), dp: 4 (over y, core).
Axes of the slice: x: 2, y: 2, z: 4, core: 2. Of those that a mesh axis runs over, the one named last changes fastest.
Arguments:
- tokens: bfloat16 [4096, 2048], P(('expert', 'dp')), may hold values from -6 to 6
- routes: int32 [4096, 8], P(('expert', 'dp')), may hold values from 0 to 63, all different within a row; in each aligned block of 128 rows (0 to 127, 128 to 255, ...) at most 32 rows name the same one
- gates: float32 [4096, 8], P(('expert', 'dp')), may hold values from 0.1 to 1
- cotangent: bfloat16 [4096, 2048], P(('expert', 'dp')), may hold values from -6 to 6
- w_up: bfloat16 [64, 2048, 128], P('expert'), may hold values from -0.125 to 0.125
- w_down: bfloat16 [64, 128, 2048], P('expert'), may hold values from -0.5 to 0.5
Outputs:
- mixed: bfloat16 [4096, 2048], P(('expert', 'dp'))
- token_grad: bfloat16 [4096, 2048], P(('expert', 'dp'))
- grad_up: bfloat16 [64, 2048, 128], P('expert', 'dp')
- grad_down: bfloat16 [64, 128, 2048], P('expert', None, 'dp')
The draws below stay inside these ranges and needn't reach their ends.
Inputs may be any that keep to these rules, and one draw needn't show every extreme that they name: `routes`: each row names 8 different experts; within the rows of one device no expert is named more than min(32, 128) times, and some expert is named exactly that often.
All inputs are finite; a program needn't handle non-finite values.
Results may differ from the reference program's by a relative error of at most 0.013.
Values may be sent and summed in bfloat16 or wider, within the bound.
A program may use at most 128 MiB of HBM per device.

```python
import math
import jax
import jax.numpy as jnp
import numpy as np
from jax import lax

D = 2048
F = 128
TOP = 8
TOK_DEV = 128
EXPERTS = 64
CAP = 16
TOKENS = 4096
N_EXPERT = 8
N_DP = 4


def level_of(own_key, extent, split, smallest, largest):
    def one(position, blocks):
        steps = jax.random.uniform(jax.random.fold_in(jax.random.fold_in(own_key, 6), position), (blocks,), jnp.float32, smallest / len(split), largest / len(split))
        return jnp.repeat(jnp.exp(steps), extent[position] // blocks).reshape((-1,) + (1,) * (len(extent) - position - 1))

    factor_of = one(*split[0])
    for cut in split[1:]:
        factor_of = factor_of * one(*cut)
    return factor_of


def shared_out(own_key, own, number, rows, count, top, bound, skew):
    order = jax.random.permutation(own_key, count)
    crowded, ordinary = portions_of(count, rows * top, bound, skew, True), portions_of(count, rows * top, bound, skew, False)
    places = jnp.arange(count)

    def named(sizes, turn):
        used = int((sizes > 0).sum())
        fixed = max(1, used // 4)
        moved = fixed + (places - fixed + turn * (used - fixed)) % max(1, count - fixed)
        return jnp.zeros((count,), jnp.int32).at[order[jnp.where(places < fixed, places, moved)]].set(jnp.asarray(sizes, jnp.int32))

    sizes = jnp.where(number % 4 == 0, named(crowded, number // 4), named(ordinary, number - number // 4 - 1))
    mixed = jax.random.permutation(jax.random.fold_in(own, 3), count)
    giver, taker = mixed[0:count // 2 * 2:2], mixed[1:count // 2 * 2:2]
    margin = jnp.minimum(sizes[giver] - 1, bound - sizes[taker]) // 2
    margin = jnp.where((giver == order[0]) | (taker == order[0]) | (sizes[taker] == 0), 0, jnp.maximum(margin, 0))
    moved = jax.random.randint(jax.random.fold_in(own, 4), (count // 2,), 0, 1 << 20) % (margin + 1)
    sizes = sizes.at[giver].add(-moved).at[taker].add(moved)
    members = jnp.searchsorted(jnp.cumsum(sizes), jnp.arange(rows * top), side="right").astype(jnp.int32)
    grid = members.reshape(top, rows).T
    grid = grid[jax.random.permutation(jax.random.fold_in(own, 1), rows)]
    turn = jax.random.randint(jax.random.fold_in(own, 2), (rows, 1), 0, top)
    return jnp.take_along_axis(grid, (jnp.arange(top)[None, :] + turn) % top, axis=1)


def portions_of(count, total, bound, lean, full):
    loads = [(1 << 20) // math.isqrt(rank ** lean) + 1 for rank in range(1, count + 1)]
    largest = bound if full else min(bound, max(-(-total // count), total * loads[0] // sum(loads)))
    least = 1 if total - largest >= count - 1 else 0
    counts, surplus = [largest] + [least] * (count - 1), total - largest - least * (count - 1)
    while surplus > 0:
        movable = [i for i in range(1, count) if counts[i] < largest] or [i for i in range(1, count) if counts[i] < bound]
        whole, left = sum([loads[i] for i in movable]), surplus
        for i in movable:
            extra = min(bound - counts[i], max(1, left * loads[i] // whole), surplus)
            counts[i] = counts[i] + extra
            surplus = surplus - extra
    return np.array(counts)


def scatter_about(rng, dims, deviation, most, shards=(), kind=jnp.bfloat16):
    factor_of = level_of(rng, dims, shards, -0.22, 0.18) if shards else 1.0
    values = jax.random.normal(rng, dims, jnp.float32) * deviation * factor_of
    return jnp.minimum(jnp.maximum(values, -most), most).astype(kind)


def setup_inputs(seed: int = 0) -> dict:
    streams_of = jax.random.split(jax.random.key(seed), 7)
    tokens = scatter_about(streams_of[0], (TOKENS, D), 1.0, 6.0, ((0, 32),))
    routes_keys = jax.random.split(jax.random.fold_in(streams_of[1], 1), TOKENS // TOK_DEV)
    routes_turns = jax.random.permutation(jax.random.fold_in(streams_of[1], 3), TOKENS // TOK_DEV)
    routes = jax.vmap(lambda own, number: shared_out(jax.random.fold_in(streams_of[1], 2), own, number, TOK_DEV, EXPERTS, TOP, min(2 * CAP, TOK_DEV), 2))(routes_keys, routes_turns).reshape((TOKENS, TOP))
    gates = jnp.clip(0.1 + 0.9 * jax.random.uniform(streams_of[2], (TOKENS, TOP), jnp.float32) ** level_of(streams_of[2], (TOKENS, TOP), ((0, 32),), -0.2, 0.2), 0.1, 1.0)
    cotangent = scatter_about(streams_of[3], (TOKENS, D), 1.0, 6.0, ((0, 32),))
    w_up = scatter_about(streams_of[4], (EXPERTS, D, F), D ** -0.5, 0.125, ((0, 8),))
    w_down = scatter_about(streams_of[5], (EXPERTS, F, D), F ** -0.5, 0.5, ((0, 8),))
    return dict(tokens=tokens, routes=routes, gates=gates, cotangent=cotangent, w_up=w_up, w_down=w_down)


gelu_coef = 0.7978845608028654
cubic_coef = 0.044715


def tanh_gelu(pre_act):
    inner_arg = gelu_coef * (pre_act + cubic_coef * pre_act * pre_act * pre_act)
    return 0.5 * pre_act * (1.0 + jnp.tanh(inner_arg))


def tanh_gelu_slope(pre_act):
    inner_arg = gelu_coef * (pre_act + cubic_coef * pre_act * pre_act * pre_act)
    tanh_part = jnp.tanh(inner_arg)
    return 0.5 * (1.0 + tanh_part) + 0.5 * pre_act * (1.0 - tanh_part * tanh_part) * gelu_coef * (1.0 + 3.0 * cubic_coef * pre_act * pre_act)


def route_ranks(flat_routes):
    positions = jnp.arange(flat_routes.shape[0], dtype=jnp.int32)
    matches = (flat_routes[None, :] == flat_routes[:, None]) & (positions[None, :] < positions[:, None])
    return jnp.sum(matches.astype(jnp.int32), axis=1)


def slot_table(flat_routes, experts_all, capacity):
    route_total = flat_routes.shape[0]
    ranking = route_ranks(flat_routes)
    kept_mask = ranking < capacity
    slot_index = jnp.where(kept_mask, flat_routes * capacity + ranking, experts_all * capacity).astype(jnp.int32)
    slot_route = jnp.full((experts_all * capacity + 1,), -1, jnp.int32)
    slot_route = slot_route.at[slot_index].set(jnp.arange(route_total, dtype=jnp.int32))
    return slot_route[:-1], kept_mask, slot_index


def reference(tokens, routes, gates, cotangent, w_up, w_down):
    block_total = N_EXPERT * N_DP
    route_block = TOK_DEV * TOP
    block_routes = routes.reshape(block_total, route_block)

    def per_block(one_block):
        slot_route, kept_mask, slot_index = slot_table(one_block, EXPERTS, CAP)
        return slot_route

    slot_route = lax.map(per_block, block_routes)
    block_base = (jnp.arange(block_total, dtype=jnp.int32) * route_block)[:, None]
    global_route = jnp.where(slot_route >= 0, slot_route + block_base, -1).astype(jnp.int32)
    per_expert = global_route.reshape(block_total, EXPERTS, CAP).transpose(1, 0, 2).reshape(EXPERTS, block_total * CAP)
    flat_gates = gates.reshape(-1)

    def expert_step(carry, inputs):
        mixed_acc, grad_acc = carry
        route_ids, up_mat, down_mat = inputs
        slot_valid = route_ids >= 0
        safe_route = jnp.where(slot_valid, route_ids, 0)
        token_ids = safe_route // TOP
        rows_in = jnp.where(slot_valid[:, None], tokens[token_ids], jnp.zeros((), jnp.bfloat16))
        gate_vals = jnp.where(slot_valid, flat_gates[safe_route], jnp.float32(0.0))
        slot_grads = (gate_vals[:, None] * cotangent[token_ids].astype(jnp.float32)).astype(jnp.bfloat16)
        pre_act = jnp.dot(rows_in, up_mat, preferred_element_type=jnp.float32)
        hidden = tanh_gelu(pre_act).astype(jnp.bfloat16)
        expert_out = jnp.dot(hidden, down_mat, preferred_element_type=jnp.float32).astype(jnp.bfloat16)
        mixed_acc = mixed_acc.at[token_ids].add(gate_vals[:, None] * expert_out.astype(jnp.float32))
        grad_hidden = jnp.dot(slot_grads, down_mat.T, preferred_element_type=jnp.float32)
        grad_pre = (grad_hidden * tanh_gelu_slope(pre_act)).astype(jnp.bfloat16)
        grad_rows = jnp.dot(grad_pre, up_mat.T, preferred_element_type=jnp.float32).astype(jnp.bfloat16)
        grad_acc = grad_acc.at[token_ids].add(grad_rows.astype(jnp.float32))
        rows_split = rows_in.reshape(N_EXPERT, N_DP, CAP, D).astype(jnp.float32)
        pre_split = grad_pre.reshape(N_EXPERT, N_DP, CAP, F).astype(jnp.float32)
        hidden_split = hidden.reshape(N_EXPERT, N_DP, CAP, F).astype(jnp.float32)
        grads_split = slot_grads.reshape(N_EXPERT, N_DP, CAP, D).astype(jnp.float32)
        part_up = jnp.einsum("apcd,apcf->pdf", rows_split, pre_split)
        part_down = jnp.einsum("apcf,apcd->pfd", hidden_split, grads_split)
        part_up = lax.optimization_barrier(part_up.astype(jnp.bfloat16))
        part_down = lax.optimization_barrier(part_down.astype(jnp.bfloat16))
        up_total = jnp.sum(part_up.astype(jnp.float32), axis=0).astype(jnp.bfloat16)
        down_total = jnp.sum(part_down.astype(jnp.float32), axis=0).astype(jnp.bfloat16)
        return (mixed_acc, grad_acc), (up_total, down_total)

    start_mixed = jnp.zeros((TOKENS, D), jnp.float32)
    start_grad = jnp.zeros((TOKENS, D), jnp.float32)
    carried, stacked = lax.scan(expert_step, (start_mixed, start_grad), (per_expert, w_up, w_down))
    mixed_acc, grad_acc = carried
    grad_up, grad_down = stacked
    mixed = (tokens.astype(jnp.float32) + mixed_acc).astype(jnp.bfloat16)
    token_grad = (cotangent.astype(jnp.float32) + grad_acc).astype(jnp.bfloat16)
    return mixed, token_grad, grad_up, grad_down
```

```python
import functools

import jax
import jax.numpy as jnp
from jax import lax
from jax.experimental import pallas as pl
from jax.experimental.pallas import tpu as pltpu
from jax.sharding import PartitionSpec as P

gelu_coef = 0.7978845608028654
cubic_coef = 0.044715
MESH = pl.DeviceIdType.MESH
CORES = 2


def gelu_and_slope(pre_act):
    square = pre_act * pre_act
    tanh_part = jnp.tanh(gelu_coef * pre_act * (1.0 + cubic_coef * square))
    value = 0.5 * pre_act * (1.0 + tanh_part)
    slope = 0.5 * (1.0 + tanh_part) + 0.5 * pre_act * (1.0 - tanh_part * tanh_part) * gelu_coef * (
        1.0 + 3.0 * cubic_coef * square
    )
    return value, slope


def kept_gates(routes, gates, experts_all, capacity):
    tok_rows = routes.shape[0]
    hits = routes[:, :, None] == jnp.arange(experts_all, dtype=jnp.int32)[None, None, :]
    named = jnp.any(hits, axis=1)
    gate_of = jnp.sum(jnp.where(hits, gates[:, :, None], jnp.float32(0.0)), axis=1)
    earlier = jnp.tril(jnp.ones((tok_rows, tok_rows), jnp.bfloat16), -1)
    rank = jnp.dot(earlier, named.astype(jnp.bfloat16), preferred_element_type=jnp.float32)
    return jnp.where(named & (rank < capacity), gate_of, jnp.float32(0.0))


def dot_nn(a, b):
    return lax.dot_general(a, b, (((1,), (0,)), ((), ())), preferred_element_type=jnp.float32)


def dot_nt(a, b):
    return lax.dot_general(a, b, (((1,), (1,)), ((), ())), preferred_element_type=jnp.float32)


class Sizes:
    def __init__(self, n_expert, n_dp, tokens, routes, w_up):
        self.n_y = n_dp // CORES
        self.n_x = n_dp // CORES
        self.n_z = n_expert // self.n_x
        self.local, self.width, self.hidden = w_up.shape
        self.rows = tokens.shape[0]
        self.top = routes.shape[1]
        self.experts = self.local * n_expert
        self.capacity = self.rows * self.top // self.experts
        self.half = self.local * self.hidden
        self.units = self.half * self.n_x
        self.column = self.rows * self.n_z
        self.slice = self.width // n_dp
        self.lanes = 2 * self.experts
        self.tile = 2 * self.hidden
        self.tiles = self.half // self.tile
        self.share = self.local // n_dp


def step_kernel(
    s,
    tok_h, routes_ref, gates_ref, cot_h, up_h, down_h,
    mixed_o, tgrad_o, gup_o, gdown_o,
    X, C, G, WU, WD, HT, GP, MS, TS, MR, TR, SB, CR, XU, YD, YU, XD,
    lsem, tok_s, tok_r, cot_s, cot_r, gate_s, gate_r, wx_s, wx_r, wy_s, wy_r, wc_s, wc_r,
    m_s, m_r, g_s, g_r, core_s, core_r, xu_s, xu_r, yd_s, yd_r, xd_s, xd_r, yu_s, yu_r,
):
    e = lax.axis_index("expert")
    p = lax.axis_index("dp")
    z, x = e // s.n_x, e % s.n_x
    y, c = p // CORES, p % CORES
    T, H, F, D = s.rows, s.half, s.hidden, s.width
    tile, tiles, sl = s.tile, s.tiles, s.slice
    wide = s.n_y * sl

    def at(z_, x_, y_, c_):
        return (z_ * s.n_x + x_, y_ * CORES + c_)

    x_peer, y_peer, c_peer = at(z, 1 - x, y, c), at(z, x, 1 - y, c), at(z, x, y, 1 - c)

    def z_peer(zz):
        return at(zz, x, y, c)

    def remote(src, dst, send, recv, device):
        return pltpu.make_async_remote_copy(
            src_ref=src, dst_ref=dst, send_sem=send, recv_sem=recv, device_id=device, device_id_type=MESH
        )

    def up(n):
        return pl.multiple_of(n, 128)

    def block(ref, zz):
        return ref.at[pl.ds(up(zz * T), T)]

    own_up = [
        pltpu.make_async_copy(up_h.at[i], WU.at[:, pl.ds(up(x * H + i * F), F)], lsem.at[2 + i])
        for i in range(s.local)
    ]
    own_down = pltpu.make_async_copy(down_h, WD.at[pl.ds(up(x * H), H)], lsem.at[2 + s.local])
    own_tok = pltpu.make_async_copy(tok_h, block(X, z), lsem.at[0])
    own_cot = pltpu.make_async_copy(cot_h, block(C, z), lsem.at[1])

    barrier = pltpu.get_barrier_semaphore()
    peers = [z_peer((z + k) % s.n_z) for k in range(1, s.n_z)] + [x_peer, y_peer, c_peer]
    for peer in peers:
        pl.semaphore_signal(barrier, inc=1, device_id=peer, device_id_type=MESH)
    own_tok.start()
    own_cot.start()
    for item in own_up:
        item.start()
    own_down.start()
    pl.semaphore_wait(barrier, len(peers))

    has_right, has_left = z < s.n_z - 1, z > 0
    right, left = jnp.minimum(z + 1, s.n_z - 1), jnp.maximum(z - 1, 0)

    def own_block(which, src, ref, send, recv, device):
        return remote(src, block(ref, z), send.at[which], recv.at[z], device)

    first_x = (y * CORES + c) * s.share

    def weight_at(u, x_, base):
        i = base + u // 2
        if u % 2 == 0:
            return WU.at[:, pl.ds(up(x_ * H + i * F), F)]
        return WD.at[pl.ds(up(x_ * H + i * F), F)]

    def weight_from(u):
        i = first_x + u // 2
        if u % 2 == 0:
            return up_h.at[i]
        return down_h.at[pl.ds(up(i * F), F)]

    n_w = 2 * s.share
    base_y = ((1 - y) * CORES + c) * s.share
    wx_send = [
        remote(weight_from(u), weight_at(u, x, first_x), wx_s.at[u], wx_r.at[u], x_peer) for u in range(n_w)
    ]
    wx_in = [
        remote(weight_from(u), weight_at(u, 1 - x, first_x), wx_s.at[u], wx_r.at[u], x_peer)
        for u in range(n_w)
    ]
    wy_send = [
        remote(weight_at(u, 1 - x, first_x), weight_at(u, 1 - x, first_x), wy_s.at[u], wy_r.at[u], y_peer)
        for u in range(n_w)
    ]
    wy_in = [
        remote(weight_at(u, 1 - x, base_y), weight_at(u, 1 - x, base_y), wy_s.at[u], wy_r.at[u], y_peer)
        for u in range(n_w)
    ]
    other_x = (y * CORES + 1 - c) * s.share
    other_y = ((1 - y) * CORES + 1 - c) * s.share
    wc_send = [
        remote(weight_at(u, 1 - x, b), weight_at(u, 1 - x, b), wc_s.at[k * n_w + u], wc_r.at[k * n_w + u], c_peer)
        for k, b in enumerate((first_x, base_y))
        for u in range(n_w)
    ]
    wc_in = [
        remote(weight_at(u, 1 - x, b), weight_at(u, 1 - x, b), wc_s.at[k * n_w + u], wc_r.at[k * n_w + u], c_peer)
        for k, b in enumerate((other_x, other_y))
        for u in range(n_w)
    ]

    @pl.when(has_right)
    def _():
        own_block(0, tok_h, X, tok_s, tok_r, z_peer(right)).start()
        own_block(0, cot_h, C, cot_s, cot_r, z_peer(right)).start()

    @pl.when(has_left)
    def _():
        own_block(1, tok_h, X, tok_s, tok_r, z_peer(left)).start()
        own_block(1, cot_h, C, cot_s, cot_r, z_peer(left)).start()

    for item in wx_send:
        item.start()

    E = s.experts
    lane = lax.broadcasted_iota(jnp.int32, (T, s.lanes), 1)
    expert = jnp.where(lane >= E, lane - E, lane)
    routes, gates = routes_ref[...], gates_ref[...]
    gate_of = jnp.zeros((T, s.lanes), jnp.float32)
    count = jnp.zeros((T, s.lanes), jnp.float32)
    for k in range(s.top):
        hit = routes[:, k : k + 1] == expert
        gate_of = gate_of + jnp.where(hit, gates[:, k : k + 1], 0.0)
        count = count + jnp.where(hit, 1.0, 0.0)
    tr = lax.broadcasted_iota(jnp.int32, (T, T), 0)
    tc = lax.broadcasted_iota(jnp.int32, (T, T), 1)
    earlier = jnp.where(tc < tr, 1.0, 0.0).astype(jnp.bfloat16)
    rank = dot_nn(earlier, count.astype(jnp.bfloat16))
    kept = jnp.where((count > 0.5) & (rank < s.capacity), gate_of, 0.0)
    high = kept.astype(jnp.bfloat16).astype(jnp.float32)
    G[pl.ds(up(z * T), T), :] = jnp.where(lane >= E, kept - high, high).astype(jnp.bfloat16)

    def gate_copy(k):
        peer = (z + k) % s.n_z
        return remote(block(G, z), block(G, z), gate_s.at[k], gate_r.at[z], z_peer(peer))

    def gate_in(zz):
        remote(block(G, zz), block(G, zz), gate_s.at[0], gate_r.at[zz], z_peer(z)).wait_recv()

    near = z + 1 - 2 * (z % 2)
    second = jnp.where(z < s.n_z // 2, s.n_z // 2, s.n_z // 2 - 1)
    last = jnp.where(z < s.n_z // 2, s.n_z - 1, 0)
    inner = has_right & has_left

    def arrive(k, src, ref, send, recv):
        remote(block(ref, src), block(ref, src), send.at[1 + k], recv.at[src], z_peer(z)).wait_recv()
        onward = jnp.where(src < z, z + 1, z - 1)
        ok = (onward >= 0) & (onward < s.n_z)
        goal = jnp.clip(onward, 0, s.n_z - 1)

        @pl.when(ok)
        def _():
            remote(block(ref, src), block(ref, src), send.at[1 + k], recv.at[src], z_peer(goal)).start()

    def arrived_sends(k, src, ref, send, recv):
        onward = jnp.where(src < z, z + 1, z - 1)
        ok = (onward >= 0) & (onward < s.n_z)

        @pl.when(ok)
        def _():
            remote(block(ref, src), block(ref, src), send.at[1 + k], recv.at[src], z_peer(z)).wait_send()

    def weight_x(u):
        wx_in[u].wait_recv()
        wy_send[u].start()
        wc_send[u].start()

    def weight_y(u):
        wy_in[u].wait_recv()
        wc_send[n_w + u].start()

    def units(row0, count_rows, tile0, n_tiles):
        rows = pl.ds(up(row0), count_rows)

        @pl.loop(0, n_tiles)
        def _(n):
            u0 = up((tile0 + n) * tile)
            cols = pl.ds(u0, tile)
            first = z * s.n_x * s.local + (tile0 + n) * (tile // F)
            ri = lax.broadcasted_iota(jnp.int32, (s.lanes, tile), 0)
            ci = lax.broadcasted_iota(jnp.int32, (s.lanes, tile), 1)
            goal = first + jnp.where(ci >= F, 1, 0)
            pick = jnp.where((ri == goal) | (ri == goal + E), 1.0, 0.0).astype(jnp.bfloat16)
            gate = dot_nn(G[rows, :], pick)
            pre = dot_nn(X[rows, :], WU[:, cols])
            value, slope = gelu_and_slope(pre)
            HT[rows, cols] = (value * gate).astype(jnp.bfloat16)
            grad_hidden = dot_nt(C[rows, :], WD[cols, :])
            GP[rows, cols] = (grad_hidden * (slope * gate)).astype(jnp.bfloat16)

    def mix(row0, count_rows):
        rows = pl.ds(up(row0), count_rows)

        @pl.loop(0, D // tile)
        def _(n):
            cols = pl.ds(up(n * tile), tile)
            MS[rows, cols] = dot_nn(HT[rows, :], WD[:, cols]).astype(jnp.bfloat16)

    def grads(row0, count_rows):
        rows = pl.ds(up(row0), count_rows)

        @pl.loop(0, D // tile)
        def _(n):
            cols = pl.ds(up(n * tile), tile)
            TS[rows, cols] = dot_nt(GP[rows, :], WU[cols, :]).astype(jnp.bfloat16)

    def give(k, dst, ref, into, send, recv):
        return remote(block(ref, dst), into.at[pl.ds(up(z * T), T)], send.at[k], recv.at[z], z_peer(dst))

    own_tok.wait()
    own_cot.wait()
    for k in range(1, s.n_z):
        gate_copy(k).start()
    for item in own_up:
        item.wait()
    own_down.wait()

    weight_x(0)
    arrive(1, near, X, tok_s, tok_r)
    weight_x(1)
    arrive(1, near, C, cot_s, cot_r)
    weight_y(0)
    arrive(2, second, X, tok_s, tok_r)
    weight_x(2)
    weight_y(1)
    arrive(2, second, C, cot_s, cot_r)
    gate_in(near)
    gate_in(second)
    gate_in(last)
    weight_x(3)
    weight_y(2)

    @pl.when(inner)
    def _():
        arrive(3, last, X, tok_s, tok_r)

    near_rows = jnp.where(z < s.n_z // 2, 0, T)
    count_rows = (s.n_z - 1) * T
    units(near_rows, count_rows, x * tiles, tiles)

    @pl.when(inner)
    def _():
        arrive(3, last, C, cot_s, cot_r)

    weight_y(3)
    for item in wc_in:
        item.wait_recv()
    units(near_rows, count_rows, (1 - x) * tiles, tiles)
    mix(near_rows, count_rows)
    give(0, near, MS, MR, m_s, m_r).start()
    give(1, second, MS, MR, m_s, m_r).start()
    grads(near_rows, count_rows)
    give(0, near, TS, TR, g_s, g_r).start()
    give(1, second, TS, TR, g_s, g_r).start()

    @pl.when(jnp.logical_not(inner))
    def _():
        arrive(3, last, X, tok_s, tok_r)
        arrive(3, last, C, cot_s, cot_r)

    units(last * T, T, 0, s.n_x * tiles)
    mix(last * T, T)
    give(2, last, MS, MR, m_s, m_r).start()

    for item in wy_send + wc_send:
        item.wait_send()
    Q = WD
    steps = s.n_x * tiles

    def unit_rows(i):
        side = jnp.where(i < tiles, 1 - x, x)
        return up(side * H + (i % tiles) * tile)

    def core_copy(i):
        rows = pl.ds(unit_rows(i), tile)
        return remote(SB.at[i % 2], CR.at[rows], core_s.at[i], core_r.at[i], c_peer)

    def xu_copy(i):
        return remote(
            Q.at[pl.ds(unit_rows(i), tile), pl.ds(0, wide)], XU.at[pl.ds(up(i * tile), tile)],
            xu_s.at[i], xu_r.at[i], x_peer,
        )

    def yd_copy(i):
        return remote(
            Q.at[pl.ds(unit_rows(i), tile), pl.ds(up(wide + (1 - y) * sl), sl)],
            YD.at[pl.ds(up(i * tile), tile)], yd_s.at[i], yd_r.at[i], y_peer,
        )

    def xd_copy(j):
        return remote(
            Q.at[pl.ds(up((1 - x) * H + j * tile), tile), pl.ds(up(wide + y * sl), sl)],
            XD.at[pl.ds(up(j * tile), tile)], xd_s.at[j], xd_r.at[j], x_peer,
        )

    def yu_copy(j):
        return remote(
            Q.at[pl.ds(up(x * H + j * tile), tile), pl.ds(up((1 - y) * sl), sl)],
            YU.at[pl.ds(up(j * tile), tile)], yu_s.at[j], yu_r.at[j], y_peer,
        )

    @pl.loop(0, steps + 1)
    def _(i):
        @pl.when(i < steps)
        def _():
            @pl.when(i >= 2)
            def _():
                core_copy(jnp.maximum(i - 2, 0)).wait_send()

            r0 = unit_rows(i)
            rows = pl.ds(r0, tile)
            slot = i % 2
            grad_t = GP[:, rows].T
            hid_t = HT[:, rows].T
            for yy in range(s.n_y):
                for arr, (left_t, right_ref) in enumerate(((grad_t, X), (hid_t, C))):
                    to = pl.ds((arr * s.n_y + yy) * sl, sl)
                    theirs = pl.ds(up((yy * CORES + 1 - c) * sl), sl)
                    mine = pl.ds(up((yy * CORES + c) * sl), sl)
                    SB[slot, :, to] = dot_nn(left_t, right_ref[:, theirs]).astype(jnp.bfloat16)
                    Q[rows, to] = dot_nn(left_t, right_ref[:, mine]).astype(jnp.bfloat16)
            core_copy(i).start()

        @pl.when(i >= 1)
        def _():
            j = jnp.maximum(i - 1, 0)
            core_copy(j).wait_recv()
            rows = pl.ds(unit_rows(j), tile)
            Q[rows, :] = (Q[rows, :].astype(jnp.float32) + CR[rows, :].astype(jnp.float32)).astype(jnp.bfloat16)

            @pl.when(j < tiles)
            def _():
                xu_copy(j).start()

            yd_copy(j).start()

    core_copy(steps - 2).wait_send()
    core_copy(steps - 1).wait_send()

    grads(last * T, T)
    give(2, last, TS, TR, g_s, g_r).start()

    @pl.loop(0, tiles)
    def _(j):
        yd_copy(j).wait_recv()
        rows = pl.ds(up((1 - x) * H + j * tile), tile)
        cols = pl.ds(up(wide + y * sl), sl)
        got = YD[pl.ds(up(j * tile), tile), :]
        Q[rows, cols] = (Q[rows, cols].astype(jnp.float32) + got.astype(jnp.float32)).astype(jnp.bfloat16)
        xd_copy(j).start()

    @pl.loop(0, tiles)
    def _(j):
        xu_copy(j).wait_recv()
        rows = pl.ds(up(x * H + j * tile), tile)
        cols = pl.ds(0, wide)
        got = XU[pl.ds(up(j * tile), tile), :]
        Q[rows, cols] = (Q[rows, cols].astype(jnp.float32) + got.astype(jnp.float32)).astype(jnp.bfloat16)
        yu_copy(j).start()

    def taken(src, into, recv):
        remote(block(into, src), block(into, src), recv.at[src], recv.at[src], z_peer(z)).wait_recv()

    def total(out, own, part, into, recv):
        for src in (near, second, last):
            taken(src, into, recv)
        value = own[pl.ds(up(z * T), T), :].astype(jnp.float32) + part[pl.ds(up(z * T), T), :].astype(jnp.float32)
        for src in (near, second, last):
            value = value + into[pl.ds(up(src * T), T), :].astype(jnp.float32)
        out[...] = value.astype(jnp.bfloat16)

    total(mixed_o, X, MS, MR, m_r)
    total(tgrad_o, C, TS, TR, g_r)

    @pl.loop(0, tiles)
    def _(j):
        yd_copy(tiles + j).wait_recv()
        xd_copy(j).wait_recv()
        rows = pl.ds(up(x * H + j * tile), tile)
        piece = pl.ds(up(j * tile), tile)
        gdown_o[piece, :] = (
            Q[rows, pl.ds(up(wide + y * sl), sl)].astype(jnp.float32)
            + YD[pl.ds(up((tiles + j) * tile), tile), :].astype(jnp.float32)
            + XD[piece, :].astype(jnp.float32)
        ).astype(jnp.bfloat16)
        yu_copy(j).wait_recv()
        gup_o[piece, :] = (
            Q[rows, pl.ds(up(y * sl), sl)].astype(jnp.float32) + YU[piece, :].astype(jnp.float32)
        ).astype(jnp.bfloat16)

    @pl.when(has_right)
    def _():
        own_block(0, tok_h, X, tok_s, tok_r, z_peer(right)).wait_send()
        own_block(0, cot_h, C, cot_s, cot_r, z_peer(right)).wait_send()

    @pl.when(has_left)
    def _():
        own_block(1, tok_h, X, tok_s, tok_r, z_peer(left)).wait_send()
        own_block(1, cot_h, C, cot_s, cot_r, z_peer(left)).wait_send()

    for k, src in ((1, near), (2, second), (3, last)):
        arrived_sends(k, src, X, tok_s, tok_r)
        arrived_sends(k, src, C, cot_s, cot_r)
    for k in range(1, s.n_z):
        gate_copy(k).wait_send()
    for item in wx_send:
        item.wait_send()
    for k, dst in ((0, near), (1, second), (2, last)):
        give(k, dst, MS, MR, m_s, m_r).wait_send()
        give(k, dst, TS, TR, g_s, g_r).wait_send()

    @pl.loop(0, tiles)
    def _(j):
        xu_copy(j).wait_send()
        xd_copy(j).wait_send()
        yu_copy(j).wait_send()

    @pl.loop(0, steps)
    def _(j):
        yd_copy(j).wait_send()


def per_device(tokens, routes, gates, cotangent, w_up, w_down):
    s = Sizes(lax.axis_size("expert"), lax.axis_size("dp"), tokens, routes, w_up)
    bf = jnp.bfloat16
    dma = pltpu.SemaphoreType.DMA
    wide = s.n_y * s.slice
    n_w = 2 * s.share
    steps = s.n_x * s.tiles
    scratch = [
        pltpu.VMEM((s.column, s.width), bf),
        pltpu.VMEM((s.column, s.width), bf),
        pltpu.VMEM((s.column, s.lanes), bf),
        pltpu.VMEM((s.width, s.units), bf),
        pltpu.VMEM((s.units, s.width), bf),
        pltpu.VMEM((s.column, s.units), bf),
        pltpu.VMEM((s.column, s.units), bf),
        pltpu.VMEM((s.column, s.width), bf),
        pltpu.VMEM((s.column, s.width), bf),
        pltpu.VMEM((s.column, s.width), bf),
        pltpu.VMEM((s.column, s.width), bf),
        pltpu.VMEM((2, s.tile, 2 * wide), bf),
        pltpu.VMEM((s.units, 2 * wide), bf),
        pltpu.VMEM((s.half, wide), bf),
        pltpu.VMEM((s.units, s.slice), bf),
        pltpu.VMEM((s.half, s.slice), bf),
        pltpu.VMEM((s.half, s.slice), bf),
        dma((3 + s.local,)),
        dma((5,)), dma((s.n_z,)), dma((5,)), dma((s.n_z,)), dma((s.n_z,)), dma((s.n_z,)),
        dma((n_w,)), dma((n_w,)), dma((n_w,)), dma((n_w,)), dma((2 * n_w,)), dma((2 * n_w,)),
        dma((3,)), dma((s.n_z,)), dma((3,)), dma((s.n_z,)),
        dma((steps,)), dma((steps,)),
        dma((s.tiles,)), dma((s.tiles,)), dma((steps,)), dma((steps,)),
        dma((s.tiles,)), dma((s.tiles,)), dma((s.tiles,)), dma((s.tiles,)),
    ]
    any_space = pl.BlockSpec(memory_space=pl.ANY)
    vmem = pl.BlockSpec(memory_space=pltpu.VMEM)
    mixed, token_grad, grad_up, grad_down = pl.pallas_call(
        functools.partial(step_kernel, s),
        out_shape=(
            jax.ShapeDtypeStruct(tokens.shape, bf),
            jax.ShapeDtypeStruct(tokens.shape, bf),
            jax.ShapeDtypeStruct((s.half, s.slice), bf),
            jax.ShapeDtypeStruct((s.half, s.slice), bf),
        ),
        in_specs=[any_space, vmem, vmem, any_space, any_space, any_space],
        out_specs=(vmem, vmem, vmem, vmem),
        scratch_shapes=scratch,
        compiler_params=pltpu.CompilerParams(
            collective_id=0, has_side_effects=True, vmem_limit_bytes=67043328
        ),
        name="moe_step",
    )(tokens, routes, gates, cotangent, w_up, w_down.reshape(s.half, s.width))
    grad_up = grad_up.reshape(s.local, s.hidden, s.slice).transpose(0, 2, 1)
    return mixed, token_grad, grad_up, grad_down.reshape(s.local, s.hidden, s.slice)


def per_device_wide(tokens, routes, gates, cotangent, w_up, w_down):
    n_expert = lax.axis_size("expert")
    local_experts, model_width, hidden_width = w_up.shape
    experts_all = local_experts * n_expert
    tok_rows = tokens.shape[0]
    top_k = routes.shape[1]
    capacity = tok_rows * top_k // experts_all
    rows_all = n_expert * tok_rows
    units = local_experts * hidden_width

    gate_full = kept_gates(routes, gates, experts_all, capacity)
    gate_hi = gate_full.astype(jnp.bfloat16)
    gate_lo = (gate_full - gate_hi.astype(jnp.float32)).astype(jnp.bfloat16)
    gate_pair = jnp.concatenate([gate_hi, gate_lo], axis=1)

    all_tokens = lax.all_gather(tokens, "expert", axis=0, tiled=True)
    all_cot = lax.all_gather(
        jnp.concatenate([cotangent, gate_pair], axis=1), "expert", axis=0, tiled=True
    )
    first = lax.axis_index("expert") * local_experts
    all_gates = lax.dynamic_slice_in_dim(
        all_cot, model_width + first, local_experts, axis=1
    ).astype(jnp.float32) + lax.dynamic_slice_in_dim(
        all_cot, model_width + experts_all + first, local_experts, axis=1
    ).astype(jnp.float32)
    all_cot = all_cot[:, :model_width]
    gate_units = all_gates[:, :, None]

    pre_act = jnp.einsum("td,edf->tef", all_tokens, w_up, preferred_element_type=jnp.float32)
    value, slope = gelu_and_slope(pre_act)
    weighted = (value * gate_units).astype(jnp.bfloat16)
    mixed_part = jnp.einsum(
        "tef,efd->td", weighted, w_down, preferred_element_type=jnp.float32
    ).astype(jnp.bfloat16)
    mixed_sum = lax.psum_scatter(mixed_part, "expert", scatter_dimension=0, tiled=True)

    grad_hidden = jnp.einsum("td,efd->tef", all_cot, w_down, preferred_element_type=jnp.float32)
    grad_pre = (grad_hidden * slope * gate_units).astype(jnp.bfloat16)
    grad_part = jnp.einsum(
        "tef,edf->td", grad_pre, w_up, preferred_element_type=jnp.float32
    ).astype(jnp.bfloat16)
    grad_sum = lax.psum_scatter(grad_part, "expert", scatter_dimension=0, tiled=True)

    part_up = jnp.einsum(
        "td,tef->edf", all_tokens, grad_pre, preferred_element_type=jnp.float32
    ).astype(jnp.bfloat16)
    part_down = jnp.einsum(
        "tef,td->efd", weighted, all_cot, preferred_element_type=jnp.float32
    ).astype(jnp.bfloat16)
    up_sum = lax.psum_scatter(part_up, "dp", scatter_dimension=1, tiled=True)
    down_sum = lax.psum_scatter(part_down, "dp", scatter_dimension=2, tiled=True)

    mixed = (tokens.astype(jnp.float32) + mixed_sum.astype(jnp.float32)).astype(jnp.bfloat16)
    token_grad = (cotangent.astype(jnp.float32) + grad_sum.astype(jnp.float32)).astype(
        jnp.bfloat16
    )
    return (mixed, token_grad, up_sum, down_sum)


def solution(mesh):
    n_expert, n_dp = mesh.shape["expert"], mesh.shape["dp"]
    small = n_expert == 8 and n_dp == 4
    return jax.shard_map(
        per_device if small else per_device_wide,
        mesh=mesh,
        in_specs=(
            P(("expert", "dp"), None),
            P(("expert", "dp"), None),
            P(("expert", "dp"), None),
            P(("expert", "dp"), None),
            P("expert", None, None),
            P("expert", None, None),
        ),
        out_specs=(
            P(("expert", "dp"), None),
            P(("expert", "dp"), None),
            P("expert", "dp", None),
            P("expert", None, "dp"),
        ),
        check_vma=False,
    )
```

```python
import functools

import jax
import jax.numpy as jnp
from jax import lax
from jax.experimental import pallas as pl
from jax.experimental.pallas import tpu as pltpu
from jax.sharding import PartitionSpec as P

gelu_coef = 0.7978845608028654
cubic_coef = 0.044715
MESH = pl.DeviceIdType.MESH
CORES = 2


def gelu_and_slope(pre_act):
    square = pre_act * pre_act
    tanh_part = jnp.tanh(gelu_coef * pre_act * (1.0 + cubic_coef * square))
    value = 0.5 * pre_act * (1.0 + tanh_part)
    slope = 0.5 * (1.0 + tanh_part) + 0.5 * pre_act * (1.0 - tanh_part * tanh_part) * gelu_coef * (
        1.0 + 3.0 * cubic_coef * square
    )
    return value, slope


def kept_gates(routes, gates, experts_all, capacity):
    tok_rows = routes.shape[0]
    hits = routes[:, :, None] == jnp.arange(experts_all, dtype=jnp.int32)[None, None, :]
    named = jnp.any(hits, axis=1)
    gate_of = jnp.sum(jnp.where(hits, gates[:, :, None], jnp.float32(0.0)), axis=1)
    earlier = jnp.tril(jnp.ones((tok_rows, tok_rows), jnp.bfloat16), -1)
    rank = jnp.dot(earlier, named.astype(jnp.bfloat16), preferred_element_type=jnp.float32)
    return jnp.where(named & (rank < capacity), gate_of, jnp.float32(0.0))


def dot_nn(a, b):
    return lax.dot_general(a, b, (((1,), (0,)), ((), ())), preferred_element_type=jnp.float32)


def dot_nt(a, b):
    return lax.dot_general(a, b, (((1,), (1,)), ((), ())), preferred_element_type=jnp.float32)


class Sizes:
    def __init__(self, n_expert, n_dp, tokens, routes, w_up):
        self.n_y = n_dp // CORES
        self.n_x = n_dp // CORES
        self.n_z = n_expert // self.n_x
        self.local, self.width, self.hidden = w_up.shape
        self.rows = tokens.shape[0]
        self.top = routes.shape[1]
        self.experts = self.local * n_expert
        self.capacity = self.rows * self.top // self.experts
        self.half = self.local * self.hidden
        self.units = self.half * self.n_x
        self.column = self.rows * self.n_z
        self.slice = self.width // n_dp
        self.lanes = 2 * self.experts
        self.tile = 2 * self.hidden
        self.tiles = self.half // self.tile
        self.share = self.local // n_dp


def step_kernel(
    s,
    tok_h, routes_h, gates_h, cot_h, up_h, down_h,
    mixed_h, tgrad_h, gup_h, gdown_h,
    X, C, G, WU, WD, HT, GP, SL, MS, TS, MN, MP, MR, TN, TP, TR, Q, SB, CR, XU, YD, YU, XD,
    mixed_o, tgrad_o, gup_o, gdown_o, routes_v, gates_v,
    lsem, osem, tok_s, tok_r, cot_s, cot_r, gate_s, gate_r, wx_s, wx_r, wy_s, wy_r, wc_s, wc_r,
    m_s, m_r, g_s, g_r, core_s, core_r, xu_s, xu_r, yd_s, yd_r, xd_s, xd_r, yu_s, yu_r,
):
    e = lax.axis_index("expert")
    p = lax.axis_index("dp")
    z, x = e // s.n_x, e % s.n_x
    y, c = p // CORES, p % CORES
    T, H, F, D = s.rows, s.half, s.hidden, s.width
    tile, tiles, sl = s.tile, s.tiles, s.slice
    steps = s.n_x * tiles
    wide = s.n_y * sl

    def at(z_, x_, y_, c_):
        return (z_ * s.n_x + x_, y_ * CORES + c_)

    x_peer, y_peer, c_peer = at(z, 1 - x, y, c), at(z, x, 1 - y, c), at(z, x, y, 1 - c)

    def z_peer(zz):
        return at(zz, x, y, c)

    def remote(src, dst, send, recv, device):
        return pltpu.make_async_remote_copy(
            src_ref=src, dst_ref=dst, send_sem=send, recv_sem=recv, device_id=device, device_id_type=MESH
        )

    def up(n):
        return pl.multiple_of(n, 128)

    def block(ref, zz):
        return ref.at[pl.ds(up(zz * T), T)]

    own_up = [
        pltpu.make_async_copy(up_h.at[i], WU.at[:, pl.ds(up(x * H + i * F), F)], lsem.at[2 + i])
        for i in range(s.local)
    ]
    own_down = pltpu.make_async_copy(down_h, WD.at[pl.ds(up(x * H), H)], lsem.at[2 + s.local])
    own_tok = pltpu.make_async_copy(tok_h, block(X, z), lsem.at[0])
    own_cot = pltpu.make_async_copy(cot_h, block(C, z), lsem.at[1])
    own_routes = pltpu.make_async_copy(routes_h, routes_v, lsem.at[3 + s.local])
    own_gates = pltpu.make_async_copy(gates_h, gates_v, lsem.at[4 + s.local])

    barrier = pltpu.get_barrier_semaphore()
    peers = [z_peer((z + k) % s.n_z) for k in range(1, s.n_z)] + [x_peer, y_peer, c_peer]
    for peer in peers:
        pl.semaphore_signal(barrier, inc=1, device_id=peer, device_id_type=MESH)
    own_routes.start()
    own_gates.start()
    own_tok.start()
    own_cot.start()
    for item in own_up:
        item.start()
    own_down.start()
    pl.semaphore_wait(barrier, len(peers))

    has_right, has_left = z < s.n_z - 1, z > 0
    right, left = jnp.minimum(z + 1, s.n_z - 1), jnp.maximum(z - 1, 0)

    def own_block(which, src, ref, send, recv, device):
        return remote(src, block(ref, z), send.at[which], recv.at[z], device)

    first_x = (y * CORES + c) * s.share

    def weight_at(u, x_, base):
        i = base + u // 2
        if u % 2 == 0:
            return WU.at[:, pl.ds(up(x_ * H + i * F), F)]
        return WD.at[pl.ds(up(x_ * H + i * F), F)]

    def weight_from(u):
        i = first_x + u // 2
        if u % 2 == 0:
            return up_h.at[i]
        return down_h.at[pl.ds(up(i * F), F)]

    n_w = 2 * s.share
    base_y = ((1 - y) * CORES + c) * s.share
    wx_send = [
        remote(weight_from(u), weight_at(u, x, first_x), wx_s.at[u], wx_r.at[u], x_peer) for u in range(n_w)
    ]
    wx_in = [
        remote(weight_from(u), weight_at(u, 1 - x, first_x), wx_s.at[u], wx_r.at[u], x_peer)
        for u in range(n_w)
    ]
    wy_send = [
        remote(weight_at(u, 1 - x, first_x), weight_at(u, 1 - x, first_x), wy_s.at[u], wy_r.at[u], y_peer)
        for u in range(n_w)
    ]
    wy_in = [
        remote(weight_at(u, 1 - x, base_y), weight_at(u, 1 - x, base_y), wy_s.at[u], wy_r.at[u], y_peer)
        for u in range(n_w)
    ]
    other_x = (y * CORES + 1 - c) * s.share
    other_y = ((1 - y) * CORES + 1 - c) * s.share
    wc_send = [
        remote(weight_at(u, 1 - x, b), weight_at(u, 1 - x, b), wc_s.at[k * n_w + u], wc_r.at[k * n_w + u], c_peer)
        for k, b in enumerate((first_x, base_y))
        for u in range(n_w)
    ]
    wc_in = [
        remote(weight_at(u, 1 - x, b), weight_at(u, 1 - x, b), wc_s.at[k * n_w + u], wc_r.at[k * n_w + u], c_peer)
        for k, b in enumerate((other_x, other_y))
        for u in range(n_w)
    ]

    @pl.when(has_right)
    def _():
        own_block(0, tok_h, X, tok_s, tok_r, z_peer(right)).start()
        own_block(0, cot_h, C, cot_s, cot_r, z_peer(right)).start()

    @pl.when(has_left)
    def _():
        own_block(1, tok_h, X, tok_s, tok_r, z_peer(left)).start()
        own_block(1, cot_h, C, cot_s, cot_r, z_peer(left)).start()

    for item in wx_send:
        item.start()

    own_routes.wait()
    own_gates.wait()
    E = s.experts
    line = lax.broadcasted_iota(jnp.int32, (s.lanes, T), 0)
    expert = jnp.where(line >= E, line - E, line)
    gate_of = jnp.zeros((s.lanes, T), jnp.float32)
    count = jnp.zeros((s.lanes, T), jnp.float32)
    for k in range(s.top):
        hit = routes_v[k : k + 1, :] == expert
        gate_of = gate_of + jnp.where(hit, gates_v[k : k + 1, :], 0.0)
        count = count + jnp.where(hit, 1.0, 0.0)
    tr = lax.broadcasted_iota(jnp.int32, (T, T), 0)
    tc = lax.broadcasted_iota(jnp.int32, (T, T), 1)
    earlier = jnp.where(tr < tc, 1.0, 0.0).astype(jnp.bfloat16)
    rank = dot_nn(count.astype(jnp.bfloat16), earlier)
    kept = jnp.where((count > 0.5) & (rank < s.capacity), gate_of, 0.0)
    high = kept.astype(jnp.bfloat16).astype(jnp.float32)
    G[pl.ds(up(z * T), T), :] = jnp.where(line >= E, kept - high, high).T.astype(jnp.bfloat16)

    def gate_copy(k):
        peer = (z + k) % s.n_z
        return remote(block(G, z), block(G, z), gate_s.at[k], gate_r.at[z], z_peer(peer))

    def gate_in(zz):
        remote(block(G, zz), block(G, zz), gate_s.at[0], gate_r.at[zz], z_peer(z)).wait_recv()

    near = z + 1 - 2 * (z % 2)
    second = jnp.where(z < s.n_z // 2, s.n_z // 2, s.n_z // 2 - 1)
    last = jnp.where(z < s.n_z // 2, s.n_z - 1, 0)
    inner = has_right & has_left

    def arrive(k, src, ref, send, recv):
        remote(block(ref, src), block(ref, src), send.at[1 + k], recv.at[src], z_peer(z)).wait_recv()
        onward = jnp.where(src < z, z + 1, z - 1)
        ok = (onward >= 0) & (onward < s.n_z)
        goal = jnp.clip(onward, 0, s.n_z - 1)

        @pl.when(ok)
        def _():
            remote(block(ref, src), block(ref, src), send.at[1 + k], recv.at[src], z_peer(goal)).start()

    def arrived_sends(k, src, ref, send, recv):
        onward = jnp.where(src < z, z + 1, z - 1)
        ok = (onward >= 0) & (onward < s.n_z)

        @pl.when(ok)
        def _():
            remote(block(ref, src), block(ref, src), send.at[1 + k], recv.at[src], z_peer(z)).wait_send()

    def weight_x(u):
        wx_in[u].wait_recv()
        wy_send[u].start()
        wc_send[u].start()

    def weight_y(u):
        wy_in[u].wait_recv()
        wc_send[n_w + u].start()

    def gate_tile(rows, t):
        first = z * s.n_x * s.local + t * (tile // F)
        ri = lax.broadcasted_iota(jnp.int32, (s.lanes, tile), 0)
        ci = lax.broadcasted_iota(jnp.int32, (s.lanes, tile), 1)
        goal = first + jnp.where(ci >= F, 1, 0)
        pick = jnp.where((ri == goal) | (ri == goal + E), 1.0, 0.0).astype(jnp.bfloat16)
        return dot_nn(G[rows, :], pick)

    def units(rows, tile0):
        @pl.loop(0, tiles)
        def _(n):
            cols = pl.ds(up((tile0 + n) * tile), tile)
            gate = gate_tile(rows, tile0 + n)
            value, slope = gelu_and_slope(dot_nn(X[rows, :], WU[:, cols]))
            HT[rows, cols] = (value * gate).astype(jnp.bfloat16)
            grad_hidden = dot_nt(C[rows, :], WD[cols, :])
            GP[rows, cols] = (grad_hidden * (slope * gate)).astype(jnp.bfloat16)

    def forward_units(rows):
        @pl.loop(0, steps)
        def _(n):
            cols = pl.ds(up(n * tile), tile)
            gate = gate_tile(rows, n)
            value, slope = gelu_and_slope(dot_nn(X[rows, :], WU[:, cols]))
            HT[rows, cols] = (value * gate).astype(jnp.bfloat16)
            SL[:, cols] = slope * gate

    def backward_units(rows):
        @pl.loop(0, steps)
        def _(n):
            cols = pl.ds(up(n * tile), tile)
            GP[rows, cols] = (dot_nt(C[rows, :], WD[cols, :]) * SL[:, cols]).astype(jnp.bfloat16)

    def mix_tile(rows, n):
        cols = pl.ds(up(n * tile), tile)
        MS[rows, cols] = dot_nn(HT[rows, :], WD[:, cols]).astype(jnp.bfloat16)

    def grad_tile(rows, n):
        cols = pl.ds(up(n * tile), tile)
        TS[rows, cols] = dot_nt(GP[rows, :], WU[cols, :]).astype(jnp.bfloat16)

    sets = ((MS, MN, MP, MR, m_s, m_r), (TS, TN, TP, TR, g_s, g_r))

    def to_near(a):
        part, into, _, _, send, recv = sets[a]
        return remote(block(part, near), into, send.at[0], recv.at[0], z_peer(near))

    def to_relay(a, k):
        part, _, _, into, send, recv = sets[a]
        return remote(block(part, (second, last)[k]), into.at[k], send.at[1 + k], recv.at[2 + k], z_peer(near))

    def to_far(a, k):
        part, _, into, _, send, recv = sets[a]
        goal = (second, last)[k]
        return remote(block(part, goal), into, send.at[1 + k], recv.at[1], z_peer(goal))

    def pass_on(a, k):
        part, _, _, into, _, _ = sets[a]
        to_relay(a, k).wait_recv()
        rows = pl.ds(up((second, last)[k] * T), T)
        part[rows, :] = part[rows, :] + into[k]
        to_far(a, k).start()

    own_tok.wait()
    own_cot.wait()
    for k in range(1, s.n_z):
        gate_copy(k).start()
    for item in own_up:
        item.wait()
    own_down.wait()

    weight_x(0)
    arrive(1, near, X, tok_s, tok_r)
    weight_x(1)
    arrive(1, near, C, cot_s, cot_r)
    weight_y(0)
    arrive(2, second, X, tok_s, tok_r)
    weight_x(2)
    weight_y(1)
    arrive(2, second, C, cot_s, cot_r)
    gate_in(near)
    gate_in(second)
    gate_in(last)
    weight_x(3)
    weight_y(2)

    @pl.when(inner)
    def _():
        arrive(3, last, X, tok_s, tok_r)

    most = pl.ds(up(jnp.where(z < s.n_z // 2, 0, T)), (s.n_z - 1) * T)
    rest = pl.ds(up(last * T), T)
    units(most, x * tiles)

    @pl.when(inner)
    def _():
        arrive(3, last, C, cot_s, cot_r)

    weight_y(3)
    for item in wc_in:
        item.wait_recv()
    units(most, (1 - x) * tiles)

    @pl.loop(0, steps)
    def _(n):
        mix_tile(most, n)

    @pl.when(jnp.logical_not(inner))
    def _():
        to_relay(0, 0).start()

    to_near(0).start()

    @pl.when(jnp.logical_not(inner))
    def _():
        arrive(3, last, X, tok_s, tok_r)

    forward_units(rest)

    @pl.when(jnp.logical_not(inner))
    def _():
        arrive(3, last, C, cot_s, cot_r)

    backward_units(rest)

    def unit_rows(i):
        side = jnp.where(i < tiles, 1 - x, x)
        return up(side * H + (i % tiles) * tile)

    def core_copy(i):
        rows = pl.ds(unit_rows(i), tile)
        return remote(SB.at[i % 2], CR.at[rows], core_s.at[i], core_r.at[i], c_peer)

    def xu_copy(i):
        return remote(
            Q.at[pl.ds(unit_rows(i), tile), pl.ds(0, wide)], XU.at[pl.ds(up(i * tile), tile)],
            xu_s.at[i], xu_r.at[i], x_peer,
        )

    def yd_copy(i):
        return remote(
            Q.at[pl.ds(unit_rows(i), tile), pl.ds(up(wide + (1 - y) * sl), sl)],
            YD.at[pl.ds(up(i * tile), tile)], yd_s.at[i], yd_r.at[i], y_peer,
        )

    def xd_copy(j):
        return remote(
            Q.at[pl.ds(up((1 - x) * H + j * tile), tile), pl.ds(up(wide + y * sl), sl)],
            XD.at[pl.ds(up(j * tile), tile)], xd_s.at[j], xd_r.at[j], x_peer,
        )

    def yu_copy(j):
        return remote(
            Q.at[pl.ds(up(x * H + j * tile), tile), pl.ds(up((1 - y) * sl), sl)],
            YU.at[pl.ds(up(j * tile), tile)], yu_s.at[j], yu_r.at[j], y_peer,
        )

    @pl.loop(0, steps + 1)
    def _(i):
        @pl.when(i < steps)
        def _():
            @pl.when(i >= 2)
            def _():
                core_copy(jnp.maximum(i - 2, 0)).wait_send()

            r0 = unit_rows(i)
            rows = pl.ds(r0, tile)
            slot = i % 2
            grad_t = GP[:, rows].T
            hid_t = HT[:, rows].T
            for yy in range(s.n_y):
                for arr, (left_t, right_ref) in enumerate(((grad_t, X), (hid_t, C))):
                    to = pl.ds((arr * s.n_y + yy) * sl, sl)
                    theirs = pl.ds(up((yy * CORES + 1 - c) * sl), sl)
                    mine = pl.ds(up((yy * CORES + c) * sl), sl)
                    SB[slot, :, to] = dot_nn(left_t, right_ref[:, theirs]).astype(jnp.bfloat16)
                    Q[rows, to] = dot_nn(left_t, right_ref[:, mine]).astype(jnp.bfloat16)
            core_copy(i).start()

        @pl.when(i >= 1)
        def _():
            j = jnp.maximum(i - 1, 0)
            core_copy(j).wait_recv()
            rows = pl.ds(unit_rows(j), tile)
            Q[rows, :] = Q[rows, :] + CR[rows, :]

            @pl.when(j < tiles)
            def _():
                xu_copy(j).start()

            yd_copy(j).start()

            @pl.when(j < tiles)
            def _():
                for k in range(s.n_x):
                    grad_tile(most, s.n_x * j + k)
                    mix_tile(rest, s.n_x * j + k)

            @pl.when(j >= tiles)
            def _():
                for k in range(s.n_x):
                    grad_tile(rest, s.n_x * (j - tiles) + k)

            @pl.when((j == tiles - 1) & inner)
            def _():
                pass_on(0, 0)
                to_near(1).start()

            @pl.when((j == tiles - 1) & jnp.logical_not(inner))
            def _():
                to_relay(1, 0).start()
                to_relay(0, 1).start()

    core_copy(steps - 2).wait_send()
    core_copy(steps - 1).wait_send()

    @pl.when(jnp.logical_not(inner))
    def _():
        to_relay(1, 1).start()
        to_near(1).start()

    @pl.when(inner)
    def _():
        pass_on(1, 0)

    @pl.loop(0, tiles)
    def _(j):
        yd_copy(j).wait_recv()
        rows = pl.ds(up((1 - x) * H + j * tile), tile)
        cols = pl.ds(up(wide + y * sl), sl)
        Q[rows, cols] = Q[rows, cols] + YD[pl.ds(up(j * tile), tile), :]
        xd_copy(j).start()

    @pl.loop(0, tiles)
    def _(j):
        xu_copy(j).wait_recv()
        rows = pl.ds(up(x * H + j * tile), tile)
        cols = pl.ds(0, wide)
        Q[rows, cols] = Q[rows, cols] + XU[pl.ds(up(j * tile), tile), :]
        yu_copy(j).start()

        @pl.when((j == tiles - 2) & inner)
        def _():
            pass_on(0, 1)

    @pl.when(inner)
    def _():
        pass_on(1, 1)

    outs = [
        pltpu.make_async_copy(a, b, osem.at[k])
        for k, (a, b) in enumerate(((mixed_o, mixed_h), (tgrad_o, tgrad_h), (gup_o, gup_h), (gdown_o, gdown_h)))
    ]

    def total(a, out, own):
        part, from_near, from_far, _, _, recv = sets[a]
        to_near(a).wait_recv()
        remote(from_far, from_far, recv.at[1], recv.at[1], z_peer(z)).wait_recv()
        rows = pl.ds(up(z * T), T)
        out[...] = (
            own[rows, :].astype(jnp.float32)
            + part[rows, :].astype(jnp.float32)
            + from_near[...].astype(jnp.float32)
            + from_far[...].astype(jnp.float32)
        ).astype(jnp.bfloat16)
        outs[a].start()

    total(0, mixed_o, X)

    @pl.loop(0, tiles)
    def _(j):
        yd_copy(tiles + j).wait_recv()
        xd_copy(j).wait_recv()
        rows = pl.ds(up(x * H + j * tile), tile)
        piece = pl.ds(up(j * tile), tile)
        gdown_o[piece, :] = (
            Q[rows, pl.ds(up(wide + y * sl), sl)].astype(jnp.float32)
            + YD[pl.ds(up((tiles + j) * tile), tile), :].astype(jnp.float32)
            + XD[piece, :].astype(jnp.float32)
        ).astype(jnp.bfloat16)
        yu_copy(j).wait_recv()
        gup_o[piece, :] = Q[rows, pl.ds(up(y * sl), sl)] + YU[piece, :]

    outs[2].start()
    outs[3].start()
    total(1, tgrad_o, C)

    @pl.when(has_right)
    def _():
        own_block(0, tok_h, X, tok_s, tok_r, z_peer(right)).wait_send()
        own_block(0, cot_h, C, cot_s, cot_r, z_peer(right)).wait_send()

    @pl.when(has_left)
    def _():
        own_block(1, tok_h, X, tok_s, tok_r, z_peer(left)).wait_send()
        own_block(1, cot_h, C, cot_s, cot_r, z_peer(left)).wait_send()

    for k, src in ((1, near), (2, second), (3, last)):
        arrived_sends(k, src, X, tok_s, tok_r)
        arrived_sends(k, src, C, cot_s, cot_r)
    for k in range(1, s.n_z):
        gate_copy(k).wait_send()
    for item in wx_send:
        item.wait_send()
    for item in wy_send + wc_send:
        item.wait_send()
    for a in range(2):
        to_near(a).wait_send()
        for k in range(2):
            to_far(a, k).wait_send()

    @pl.loop(0, tiles)
    def _(j):
        xu_copy(j).wait_send()
        xd_copy(j).wait_send()
        yu_copy(j).wait_send()

    @pl.loop(0, steps)
    def _(j):
        yd_copy(j).wait_send()

    for item in outs:
        item.wait()


def finish_kernel(
    mixed_h, tgrad_h, gup_h, gdown_h, mixed_f, tgrad_f, gup_f, gdown_f, mixed_v, tgrad_v, gup_v, gdown_v, turned, into, out
):
    copies = []
    for k, (a, b) in enumerate(((gup_h, gup_v), (mixed_h, mixed_v), (tgrad_h, tgrad_v), (gdown_h, gdown_v))):
        copies.append(pltpu.make_async_copy(a, b, into.at[k]))
        copies[-1].start()
    back = [
        pltpu.make_async_copy(a, b, out.at[k])
        for k, (a, b) in enumerate(((turned, gup_f), (mixed_v, mixed_f), (tgrad_v, tgrad_f), (gdown_v, gdown_f)))
    ]
    copies[0].wait()
    for i in range(gup_v.shape[0]):
        turned[i] = gup_v[i].T
    for k in range(1, 4):
        copies[k].wait()
        back[k].start()
    back[0].start()
    for item in back:
        item.wait()


def per_device(tokens, routes, gates, cotangent, w_up, w_down):
    s = Sizes(lax.axis_size("expert"), lax.axis_size("dp"), tokens, routes, w_up)
    bf = jnp.bfloat16
    dma = pltpu.SemaphoreType.DMA
    wide = s.n_y * s.slice
    n_w = 2 * s.share
    steps = s.n_x * s.tiles
    block = (s.rows, s.width)
    scratch = [
        pltpu.VMEM((s.column, s.width), bf),
        pltpu.VMEM((s.column, s.width), bf),
        pltpu.VMEM((s.column, s.lanes), bf),
        pltpu.VMEM((s.width, s.units), bf),
        pltpu.VMEM((s.units, s.width), bf),
        pltpu.VMEM((s.column, s.units), bf),
        pltpu.VMEM((s.column, s.units), bf),
        pltpu.VMEM((s.rows, s.units), jnp.float32),
        pltpu.VMEM((s.column, s.width), bf),
        pltpu.VMEM((s.column, s.width), bf),
        pltpu.VMEM(block, bf), pltpu.VMEM(block, bf), pltpu.VMEM((2,) + block, bf),
        pltpu.VMEM(block, bf), pltpu.VMEM(block, bf), pltpu.VMEM((2,) + block, bf),
        pltpu.VMEM((s.units, 2 * wide), bf),
        pltpu.VMEM((2, s.tile, 2 * wide), bf),
        pltpu.VMEM((s.units, 2 * wide), bf),
        pltpu.VMEM((s.half, wide), bf),
        pltpu.VMEM((s.units, s.slice), bf),
        pltpu.VMEM((s.half, s.slice), bf),
        pltpu.VMEM((s.half, s.slice), bf),
        pltpu.VMEM(block, bf), pltpu.VMEM(block, bf),
        pltpu.VMEM((s.half, s.slice), bf), pltpu.VMEM((s.half, s.slice), bf),
        pltpu.VMEM((s.top, s.rows), jnp.int32), pltpu.VMEM((s.top, s.rows), jnp.float32),
        dma((5 + s.local,)), dma((4,)),
        dma((5,)), dma((s.n_z,)), dma((5,)), dma((s.n_z,)), dma((s.n_z,)), dma((s.n_z,)),
        dma((n_w,)), dma((n_w,)), dma((n_w,)), dma((n_w,)), dma((2 * n_w,)), dma((2 * n_w,)),
        dma((3,)), dma((4,)), dma((3,)), dma((4,)),
        dma((steps,)), dma((steps,)),
        dma((s.tiles,)), dma((s.tiles,)), dma((steps,)), dma((steps,)),
        dma((s.tiles,)), dma((s.tiles,)), dma((s.tiles,)), dma((s.tiles,)),
    ]
    any_space = pl.BlockSpec(memory_space=pl.ANY)
    parts = pl.pallas_call(
        functools.partial(step_kernel, s),
        out_shape=(
            jax.ShapeDtypeStruct(tokens.shape, bf),
            jax.ShapeDtypeStruct(tokens.shape, bf),
            jax.ShapeDtypeStruct((s.half, s.slice), bf),
            jax.ShapeDtypeStruct((s.half, s.slice), bf),
        ),
        in_specs=[any_space] * 6,
        out_specs=(any_space,) * 4,
        scratch_shapes=scratch,
        compiler_params=pltpu.CompilerParams(
            collective_id=0, has_side_effects=True, vmem_limit_bytes=67043328
        ),
        name="moe_step",
    )(tokens, routes.T, gates.T, cotangent, w_up, w_down.reshape(s.half, s.width))
    shapes = (
        tokens.shape,
        tokens.shape,
        (s.local, s.slice, s.hidden),
        (s.local, s.hidden, s.slice),
    )
    turned = (s.local, s.hidden, s.slice)
    mixed, token_grad, grad_up, grad_down = parts
    return pl.pallas_call(
        finish_kernel,
        out_shape=tuple(jax.ShapeDtypeStruct(shape, bf) for shape in shapes),
        in_specs=[any_space] * 4,
        out_specs=(any_space,) * 4,
        scratch_shapes=[
            pltpu.VMEM(tokens.shape, bf),
            pltpu.VMEM(tokens.shape, bf),
            pltpu.VMEM(turned, bf),
            pltpu.VMEM(turned, bf),
            pltpu.VMEM(shapes[2], bf),
            dma((4,)),
            dma((4,)),
        ],
        name="finish",
    )(mixed, token_grad, grad_up.reshape(turned), grad_down.reshape(turned))


def per_device_wide(tokens, routes, gates, cotangent, w_up, w_down):
    n_expert = lax.axis_size("expert")
    local_experts, model_width, hidden_width = w_up.shape
    experts_all = local_experts * n_expert
    tok_rows = tokens.shape[0]
    top_k = routes.shape[1]
    capacity = tok_rows * top_k // experts_all
    rows_all = n_expert * tok_rows
    units = local_experts * hidden_width

    gate_full = kept_gates(routes, gates, experts_all, capacity)
    gate_hi = gate_full.astype(jnp.bfloat16)
    gate_lo = (gate_full - gate_hi.astype(jnp.float32)).astype(jnp.bfloat16)
    gate_pair = jnp.concatenate([gate_hi, gate_lo], axis=1)

    all_tokens = lax.all_gather(tokens, "expert", axis=0, tiled=True)
    all_cot = lax.all_gather(
        jnp.concatenate([cotangent, gate_pair], axis=1), "expert", axis=0, tiled=True
    )
    first = lax.axis_index("expert") * local_experts
    all_gates = lax.dynamic_slice_in_dim(
        all_cot, model_width + first, local_experts, axis=1
    ).astype(jnp.float32) + lax.dynamic_slice_in_dim(
        all_cot, model_width + experts_all + first, local_experts, axis=1
    ).astype(jnp.float32)
    all_cot = all_cot[:, :model_width]
    gate_units = all_gates[:, :, None]

    pre_act = jnp.einsum("td,edf->tef", all_tokens, w_up, preferred_element_type=jnp.float32)
    value, slope = gelu_and_slope(pre_act)
    weighted = (value * gate_units).astype(jnp.bfloat16)
    mixed_part = jnp.einsum(
        "tef,efd->td", weighted, w_down, preferred_element_type=jnp.float32
    ).astype(jnp.bfloat16)
    mixed_sum = lax.psum_scatter(mixed_part, "expert", scatter_dimension=0, tiled=True)

    grad_hidden = jnp.einsum("td,efd->tef", all_cot, w_down, preferred_element_type=jnp.float32)
    grad_pre = (grad_hidden * slope * gate_units).astype(jnp.bfloat16)
    grad_part = jnp.einsum(
        "tef,edf->td", grad_pre, w_up, preferred_element_type=jnp.float32
    ).astype(jnp.bfloat16)
    grad_sum = lax.psum_scatter(grad_part, "expert", scatter_dimension=0, tiled=True)

    part_up = jnp.einsum(
        "td,tef->edf", all_tokens, grad_pre, preferred_element_type=jnp.float32
    ).astype(jnp.bfloat16)
    part_down = jnp.einsum(
        "tef,td->efd", weighted, all_cot, preferred_element_type=jnp.float32
    ).astype(jnp.bfloat16)
    up_sum = lax.psum_scatter(part_up, "dp", scatter_dimension=1, tiled=True)
    down_sum = lax.psum_scatter(part_down, "dp", scatter_dimension=2, tiled=True)

    mixed = (tokens.astype(jnp.float32) + mixed_sum.astype(jnp.float32)).astype(jnp.bfloat16)
    token_grad = (cotangent.astype(jnp.float32) + grad_sum.astype(jnp.float32)).astype(
        jnp.bfloat16
    )
    return (mixed, token_grad, up_sum, down_sum)


def solution(mesh):
    n_expert, n_dp = mesh.shape["expert"], mesh.shape["dp"]
    small = n_expert == 8 and n_dp == 4
    return jax.shard_map(
        per_device if small else per_device_wide,
        mesh=mesh,
        in_specs=(
            P(("expert", "dp"), None),
            P(("expert", "dp"), None),
            P(("expert", "dp"), None),
            P(("expert", "dp"), None),
            P("expert", None, None),
            P("expert", None, None),
        ),
        out_specs=(
            P(("expert", "dp"), None),
            P(("expert", "dp"), None),
            P("expert", "dp", None),
            P("expert", None, "dp"),
        ),
        check_vma=False,
    )
```

```python
import functools

import jax
import jax.numpy as jnp
from jax import lax
from jax.experimental import pallas as pl
from jax.experimental.pallas import tpu as pltpu
from jax.sharding import PartitionSpec as P

gelu_coef = 0.7978845608028654
cubic_coef = 0.044715
MESH = pl.DeviceIdType.MESH
CORES = 2


def gelu_and_slope(pre_act):
    square = pre_act * pre_act
    tanh_part = jnp.tanh(gelu_coef * pre_act * (1.0 + cubic_coef * square))
    value = 0.5 * pre_act * (1.0 + tanh_part)
    slope = 0.5 * (1.0 + tanh_part) + 0.5 * pre_act * (1.0 - tanh_part * tanh_part) * gelu_coef * (
        1.0 + 3.0 * cubic_coef * square
    )
    return value, slope


def kept_gates(routes, gates, experts_all, capacity):
    tok_rows = routes.shape[0]
    hits = routes[:, :, None] == jnp.arange(experts_all, dtype=jnp.int32)[None, None, :]
    named = jnp.any(hits, axis=1)
    gate_of = jnp.sum(jnp.where(hits, gates[:, :, None], jnp.float32(0.0)), axis=1)
    earlier = jnp.tril(jnp.ones((tok_rows, tok_rows), jnp.bfloat16), -1)
    rank = jnp.dot(earlier, named.astype(jnp.bfloat16), preferred_element_type=jnp.float32)
    return jnp.where(named & (rank < capacity), gate_of, jnp.float32(0.0))


def dot_nn(a, b):
    return lax.dot_general(a, b, (((1,), (0,)), ((), ())), preferred_element_type=jnp.float32)


def dot_nt(a, b):
    return lax.dot_general(a, b, (((1,), (1,)), ((), ())), preferred_element_type=jnp.float32)


class Sizes:
    def __init__(self, n_expert, n_dp, tokens, routes, w_up):
        self.n_y = n_dp // CORES
        self.n_x = n_dp // CORES
        self.n_z = n_expert // self.n_x
        self.local, self.width, self.hidden = w_up.shape
        self.rows = tokens.shape[0]
        self.top = routes.shape[1]
        self.experts = self.local * n_expert
        self.capacity = self.rows * self.top // self.experts
        self.half = self.local * self.hidden
        self.units = self.half * self.n_x
        self.column = self.rows * self.n_z
        self.slice = self.width // n_dp
        self.lanes = 2 * self.experts
        self.tile = 2 * self.hidden
        self.tiles = self.half // self.tile
        self.share = self.local // n_dp


def step_kernel(
    s,
    tok_h, routes_h, gates_h, cot_h, up_h, down_h,
    mixed_h, tgrad_h, gup_h, gdown_h,
    X, C, G, WU, WD, HT, GP, SL, MS, TS, MN, MP, MR, TN, TP, TR, Q, SB, CR, XU, YD, YU, XD,
    mixed_o, tgrad_o, gup_o, gdown_o, routes_v, gates_v,
    lsem, osem, tok_s, tok_r, cot_s, cot_r, gate_s, gate_r, wx_s, wx_r, wy_s, wy_r, wc_s, wc_r,
    m_s, m_r, g_s, g_r, core_s, core_r, xu_s, xu_r, yd_s, yd_r, xd_s, xd_r, yu_s, yu_r,
):
    e = lax.axis_index("expert")
    p = lax.axis_index("dp")
    z, x = e // s.n_x, e % s.n_x
    y, c = p // CORES, p % CORES
    T, H, F, D = s.rows, s.half, s.hidden, s.width
    tile, tiles, sl = s.tile, s.tiles, s.slice
    steps = s.n_x * tiles
    wide = s.n_y * sl

    def at(z_, x_, y_, c_):
        return (z_ * s.n_x + x_, y_ * CORES + c_)

    x_peer, y_peer, c_peer = at(z, 1 - x, y, c), at(z, x, 1 - y, c), at(z, x, y, 1 - c)

    def z_peer(zz):
        return at(zz, x, y, c)

    def remote(src, dst, send, recv, device):
        return pltpu.make_async_remote_copy(
            src_ref=src, dst_ref=dst, send_sem=send, recv_sem=recv, device_id=device, device_id_type=MESH
        )

    def up(n):
        return pl.multiple_of(n, 128)

    def block(ref, zz):
        return ref.at[pl.ds(up(zz * T), T)]

    own_up = [
        pltpu.make_async_copy(up_h.at[i], WU.at[:, pl.ds(up(x * H + i * F), F)], lsem.at[2 + i])
        for i in range(s.local)
    ]
    own_down = pltpu.make_async_copy(down_h, WD.at[pl.ds(up(x * H), H)], lsem.at[2 + s.local])
    own_tok = pltpu.make_async_copy(tok_h, block(X, z), lsem.at[0])
    own_cot = pltpu.make_async_copy(cot_h, block(C, z), lsem.at[1])
    own_routes = pltpu.make_async_copy(routes_h, routes_v, lsem.at[3 + s.local])
    own_gates = pltpu.make_async_copy(gates_h, gates_v, lsem.at[4 + s.local])

    barrier = pltpu.get_barrier_semaphore()
    peers = [z_peer((z + k) % s.n_z) for k in range(1, s.n_z)] + [x_peer, y_peer, c_peer]
    for peer in peers:
        pl.semaphore_signal(barrier, inc=1, device_id=peer, device_id_type=MESH)
    own_routes.start()
    own_gates.start()
    own_tok.start()
    own_cot.start()
    for item in own_up:
        item.start()
    own_down.start()
    pl.semaphore_wait(barrier, len(peers))

    has_right, has_left = z < s.n_z - 1, z > 0
    right, left = jnp.minimum(z + 1, s.n_z - 1), jnp.maximum(z - 1, 0)

    def own_block(which, src, ref, send, recv, device):
        return remote(src, block(ref, z), send.at[which], recv.at[z], device)

    first_x = (y * CORES + c) * s.share

    def weight_at(u, x_, base):
        i, half = base + u // 4, u % 2
        if u % 4 < 2:
            return WU.at[pl.ds(half * (D // 2), D // 2), pl.ds(up(x_ * H + i * F), F)]
        return WD.at[pl.ds(pl.multiple_of(x_ * H + i * F + half * (F // 2), F // 2), F // 2)]

    def weight_from(u):
        i, half = first_x + u // 4, u % 2
        if u % 4 < 2:
            return up_h.at[i, pl.ds(half * (D // 2), D // 2)]
        return down_h.at[pl.ds(pl.multiple_of(i * F + half * (F // 2), F // 2), F // 2)]

    n_w = 4 * s.share
    base_y = ((1 - y) * CORES + c) * s.share
    wx_send = [
        remote(weight_from(u), weight_at(u, x, first_x), wx_s.at[u], wx_r.at[u], x_peer) for u in range(n_w)
    ]
    wx_in = [
        remote(weight_from(u), weight_at(u, 1 - x, first_x), wx_s.at[u], wx_r.at[u], x_peer)
        for u in range(n_w)
    ]
    wy_send = [
        remote(weight_at(u, 1 - x, first_x), weight_at(u, 1 - x, first_x), wy_s.at[u], wy_r.at[u], y_peer)
        for u in range(n_w)
    ]
    wy_in = [
        remote(weight_at(u, 1 - x, base_y), weight_at(u, 1 - x, base_y), wy_s.at[u], wy_r.at[u], y_peer)
        for u in range(n_w)
    ]
    other_x = (y * CORES + 1 - c) * s.share
    other_y = ((1 - y) * CORES + 1 - c) * s.share
    wc_send = [
        remote(weight_at(u, 1 - x, b), weight_at(u, 1 - x, b), wc_s.at[k * n_w + u], wc_r.at[k * n_w + u], c_peer)
        for k, b in enumerate((first_x, base_y))
        for u in range(n_w)
    ]
    wc_in = [
        remote(weight_at(u, 1 - x, b), weight_at(u, 1 - x, b), wc_s.at[k * n_w + u], wc_r.at[k * n_w + u], c_peer)
        for k, b in enumerate((other_x, other_y))
        for u in range(n_w)
    ]

    @pl.when(has_right)
    def _():
        own_block(0, tok_h, X, tok_s, tok_r, z_peer(right)).start()
        own_block(0, cot_h, C, cot_s, cot_r, z_peer(right)).start()

    @pl.when(has_left)
    def _():
        own_block(1, tok_h, X, tok_s, tok_r, z_peer(left)).start()
        own_block(1, cot_h, C, cot_s, cot_r, z_peer(left)).start()

    for item in wx_send:
        item.start()

    own_routes.wait()
    own_gates.wait()
    E = s.experts
    line = lax.broadcasted_iota(jnp.int32, (s.lanes, T), 0)
    expert = jnp.where(line >= E, line - E, line)
    gate_of = jnp.zeros((s.lanes, T), jnp.float32)
    count = jnp.zeros((s.lanes, T), jnp.float32)
    for k in range(s.top):
        hit = routes_v[k : k + 1, :] == expert
        gate_of = gate_of + jnp.where(hit, gates_v[k : k + 1, :], 0.0)
        count = count + jnp.where(hit, 1.0, 0.0)
    tr = lax.broadcasted_iota(jnp.int32, (T, T), 0)
    tc = lax.broadcasted_iota(jnp.int32, (T, T), 1)
    earlier = jnp.where(tr < tc, 1.0, 0.0).astype(jnp.bfloat16)
    rank = dot_nn(count.astype(jnp.bfloat16), earlier)
    kept = jnp.where((count > 0.5) & (rank < s.capacity), gate_of, 0.0)
    high = kept.astype(jnp.bfloat16).astype(jnp.float32)
    G[pl.ds(up(z * T), T), :] = jnp.where(line >= E, kept - high, high).T.astype(jnp.bfloat16)

    def gate_copy(k):
        peer = (z + k) % s.n_z
        return remote(block(G, z), block(G, z), gate_s.at[k], gate_r.at[z], z_peer(peer))

    def gate_in(zz):
        remote(block(G, zz), block(G, zz), gate_s.at[0], gate_r.at[zz], z_peer(z)).wait_recv()

    near = z + 1 - 2 * (z % 2)
    second = jnp.where(z < s.n_z // 2, s.n_z // 2, s.n_z // 2 - 1)
    last = jnp.where(z < s.n_z // 2, s.n_z - 1, 0)
    inner = has_right & has_left

    def arrive(k, src, ref, send, recv):
        remote(block(ref, src), block(ref, src), send.at[1 + k], recv.at[src], z_peer(z)).wait_recv()
        onward = jnp.where(src < z, z + 1, z - 1)
        ok = (onward >= 0) & (onward < s.n_z)
        goal = jnp.clip(onward, 0, s.n_z - 1)

        @pl.when(ok)
        def _():
            remote(block(ref, src), block(ref, src), send.at[1 + k], recv.at[src], z_peer(goal)).start()

    def arrived_sends(k, src, ref, send, recv):
        onward = jnp.where(src < z, z + 1, z - 1)
        ok = (onward >= 0) & (onward < s.n_z)

        @pl.when(ok)
        def _():
            remote(block(ref, src), block(ref, src), send.at[1 + k], recv.at[src], z_peer(z)).wait_send()

    def weight_x(u):
        wx_in[u].wait_recv()
        wy_send[u].start()
        wc_send[u].start()

    def weight_y(u):
        wy_in[u].wait_recv()
        wc_send[n_w + u].start()

    def gate_tile(rows, t):
        first = z * s.n_x * s.local + t * (tile // F)
        ri = lax.broadcasted_iota(jnp.int32, (s.lanes, tile), 0)
        ci = lax.broadcasted_iota(jnp.int32, (s.lanes, tile), 1)
        goal = first + jnp.where(ci >= F, 1, 0)
        pick = jnp.where((ri == goal) | (ri == goal + E), 1.0, 0.0).astype(jnp.bfloat16)
        return dot_nn(G[rows, :], pick)

    def units(rows, tile0):
        @pl.loop(0, tiles)
        def _(n):
            cols = pl.ds(up((tile0 + n) * tile), tile)
            gate = gate_tile(rows, tile0 + n)
            value, slope = gelu_and_slope(dot_nn(X[rows, :], WU[:, cols]))
            HT[rows, cols] = (value * gate).astype(jnp.bfloat16)
            grad_hidden = dot_nt(C[rows, :], WD[cols, :])
            GP[rows, cols] = (grad_hidden * (slope * gate)).astype(jnp.bfloat16)

    def forward_units(rows):
        @pl.loop(0, steps)
        def _(n):
            cols = pl.ds(up(n * tile), tile)
            gate = gate_tile(rows, n)
            value, slope = gelu_and_slope(dot_nn(X[rows, :], WU[:, cols]))
            HT[rows, cols] = (value * gate).astype(jnp.bfloat16)
            SL[:, cols] = slope * gate

    def backward_tile(rows, u0):
        cols = pl.ds(u0, tile)
        GP[rows, cols] = (dot_nt(C[rows, :], WD[cols, :]) * SL[:, cols]).astype(jnp.bfloat16)

    def mix_tile(rows, n):
        cols = pl.ds(up(n * tile), tile)
        MS[rows, cols] = dot_nn(HT[rows, :], WD[:, cols]).astype(jnp.bfloat16)

    def grad_tile(rows, n):
        cols = pl.ds(up(n * tile), tile)
        TS[rows, cols] = dot_nt(GP[rows, :], WU[cols, :]).astype(jnp.bfloat16)

    def mix_side(rows, side, add):
        inner_cols = pl.ds(up(side * H), H)

        @pl.loop(0, steps)
        def _(n):
            cols = pl.ds(up(n * tile), tile)
            value = dot_nn(HT[rows, inner_cols], WD[inner_cols, cols])
            if add:
                value = value + MS[rows, cols].astype(jnp.float32)
            MS[rows, cols] = value.astype(jnp.bfloat16)

    def grad_side(rows, side):
        inner_cols = pl.ds(up(side * H), H)

        @pl.loop(0, steps)
        def _(n):
            cols = pl.ds(up(n * tile), tile)
            TS[rows, cols] = dot_nt(GP[rows, inner_cols], WU[cols, inner_cols]).astype(jnp.bfloat16)

    def grad_rest_tile(rows, side, n):
        inner_cols = pl.ds(up(side * H), H)
        cols = pl.ds(up(n * tile), tile)
        value = dot_nt(GP[rows, inner_cols], WU[cols, inner_cols]) + TS[rows, cols].astype(jnp.float32)
        TS[rows, cols] = value.astype(jnp.bfloat16)

    sets = ((MS, MN, MP, MR, m_s, m_r), (TS, TN, TP, TR, g_s, g_r))

    def to_near(a):
        part, into, _, _, send, recv = sets[a]
        return remote(block(part, near), into, send.at[0], recv.at[0], z_peer(near))

    def to_relay(a, k):
        part, _, _, into, send, recv = sets[a]
        return remote(block(part, (second, last)[k]), into.at[k], send.at[1 + k], recv.at[2 + k], z_peer(near))

    def to_far(a, k):
        part, _, into, _, send, recv = sets[a]
        goal = (second, last)[k]
        return remote(block(part, goal), into, send.at[1 + k], recv.at[1], z_peer(goal))

    def pass_on(a, k):
        part, _, _, into, _, _ = sets[a]
        to_relay(a, k).wait_recv()
        rows = pl.ds(up((second, last)[k] * T), T)
        part[rows, :] = part[rows, :] + into[k]
        to_far(a, k).start()

    own_tok.wait()
    own_cot.wait()
    for k in range(1, s.n_z):
        gate_copy(k).start()
    for item in own_up:
        item.wait()
    own_down.wait()

    low = z < s.n_z // 2
    pair = pl.ds(up(jnp.where(low, 0, 2 * T)), 2 * T)
    single = pl.ds(up(second * T), T)
    most = pl.ds(up(jnp.where(low, 0, T)), (s.n_z - 1) * T)
    rest = pl.ds(up(last * T), T)

    weight_x(0)
    weight_x(1)
    arrive(1, near, X, tok_s, tok_r)
    weight_y(0)
    weight_x(2)
    weight_y(1)
    weight_x(3)
    arrive(1, near, C, cot_s, cot_r)
    weight_y(2)

    @pl.when(inner)
    def _():
        arrive(2, second, X, tok_s, tok_r)

    gate_in(near)
    units(pair, x * tiles)
    weight_x(4)
    weight_y(3)
    mix_side(pair, x, False)

    @pl.when(inner)
    def _():
        arrive(2, second, C, cot_s, cot_r)

    grad_side(pair, x)
    weight_x(5)
    weight_y(4)

    @pl.when(jnp.logical_not(inner))
    def _():
        arrive(2, second, X, tok_s, tok_r)

    weight_x(6)
    weight_y(5)

    @pl.when(inner)
    def _():
        arrive(3, last, X, tok_s, tok_r)

    @pl.when(jnp.logical_not(inner))
    def _():
        arrive(2, second, C, cot_s, cot_r)

    weight_x(7)
    weight_y(6)
    gate_in(second)
    gate_in(last)
    units(single, x * tiles)
    mix_side(single, x, False)
    grad_side(single, x)

    @pl.when(inner)
    def _():
        arrive(3, last, C, cot_s, cot_r)

    weight_y(7)
    for item in wc_in:
        item.wait_recv()
    units(most, (1 - x) * tiles)
    mix_side(most, 1 - x, True)

    @pl.when(jnp.logical_not(inner))
    def _():
        to_relay(0, 0).start()

    to_near(0).start()

    @pl.when(jnp.logical_not(inner))
    def _():
        arrive(3, last, X, tok_s, tok_r)

    forward_units(rest)

    @pl.when(jnp.logical_not(inner))
    def _():
        arrive(3, last, C, cot_s, cot_r)

    def unit_rows(i):
        side = jnp.where(i < tiles, 1 - x, x)
        return up(side * H + (i % tiles) * tile)

    def core_copy(i, arr):
        rows, cols = pl.ds(unit_rows(i), tile), pl.ds(arr * wide, wide)
        return remote(
            SB.at[i % 2, :, cols], CR.at[rows, cols],
            core_s.at[arr * steps + i], core_r.at[arr * steps + i], c_peer,
        )

    def xu_copy(i):
        return remote(
            Q.at[pl.ds(unit_rows(i), tile), pl.ds(0, wide)], XU.at[pl.ds(up(i * tile), tile)],
            xu_s.at[i], xu_r.at[i], x_peer,
        )

    def yd_copy(i):
        return remote(
            Q.at[pl.ds(unit_rows(i), tile), pl.ds(up(wide + (1 - y) * sl), sl)],
            YD.at[pl.ds(up(i * tile), tile)], yd_s.at[i], yd_r.at[i], y_peer,
        )

    def xd_copy(j):
        return remote(
            Q.at[pl.ds(up((1 - x) * H + j * tile), tile), pl.ds(up(wide + y * sl), sl)],
            XD.at[pl.ds(up(j * tile), tile)], xd_s.at[j], xd_r.at[j], x_peer,
        )

    def yu_copy(j):
        return remote(
            Q.at[pl.ds(up(x * H + j * tile), tile), pl.ds(up((1 - y) * sl), sl)],
            YU.at[pl.ds(up(j * tile), tile)], yu_s.at[j], yu_r.at[j], y_peer,
        )

    def give_part(i, arr, left_ref, right_ref):
        @pl.when(i >= 2)
        def _():
            core_copy(jnp.maximum(i - 2, 0), arr).wait_send()

        left_t = left_ref[:, pl.ds(unit_rows(i), tile)].T
        for yy in range(s.n_y):
            to = pl.ds((arr * s.n_y + yy) * sl, sl)
            theirs = pl.ds(up((yy * CORES + 1 - c) * sl), sl)
            SB[i % 2, :, to] = dot_nn(left_t, right_ref[:, theirs]).astype(jnp.bfloat16)
        core_copy(i, arr).start()
        return left_t

    def keep_part(i, arr, left_t, right_ref):
        rows = pl.ds(unit_rows(i), tile)
        for yy in range(s.n_y):
            to = pl.ds((arr * s.n_y + yy) * sl, sl)
            mine = pl.ds(up((yy * CORES + c) * sl), sl)
            Q[rows, to] = dot_nn(left_t, right_ref[:, mine]).astype(jnp.bfloat16)

    def join(i, arr):
        core_copy(i, arr).wait_recv()
        rows, cols = pl.ds(unit_rows(i), tile), pl.ds(arr * wide, wide)
        Q[rows, cols] = Q[rows, cols] + CR[rows, cols]

    @pl.loop(0, steps)
    def _(i):
        hid_t = give_part(i, 1, HT, C)
        backward_tile(rest, unit_rows(i))
        grad_t = give_part(i, 0, GP, X)
        keep_part(i, 1, hid_t, C)
        join(i, 1)
        yd_copy(i).start()
        keep_part(i, 0, grad_t, X)
        join(i, 0)

        @pl.when(i < tiles)
        def _():
            xu_copy(i).start()
            for k in range(s.n_x):
                grad_rest_tile(most, 1 - x, s.n_x * i + k)

        @pl.when(i >= tiles)
        def _():
            for k in range(s.n_x):
                mix_tile(rest, s.n_x * (i - tiles) + k)

        @pl.when((i == tiles - 1) & inner)
        def _():
            to_near(1).start()
            pass_on(0, 0)

        @pl.when((i == tiles - 1) & jnp.logical_not(inner))
        def _():
            to_relay(1, 0).start()

    for k in range(2):
        core_copy(steps - 2 + k, 0).wait_send()
        core_copy(steps - 2 + k, 1).wait_send()

    @pl.when(jnp.logical_not(inner))
    def _():
        to_relay(0, 1).start()

    @pl.loop(0, steps)
    def _(n):
        grad_tile(rest, n)

    @pl.when(jnp.logical_not(inner))
    def _():
        to_relay(1, 1).start()
        to_near(1).start()

    @pl.when(inner)
    def _():
        pass_on(1, 0)

    @pl.loop(0, tiles)
    def _(j):
        yd_copy(j).wait_recv()
        rows = pl.ds(up((1 - x) * H + j * tile), tile)
        cols = pl.ds(up(wide + y * sl), sl)
        Q[rows, cols] = Q[rows, cols] + YD[pl.ds(up(j * tile), tile), :]
        xd_copy(j).start()

    @pl.loop(0, tiles)
    def _(j):
        xu_copy(j).wait_recv()
        rows = pl.ds(up(x * H + j * tile), tile)
        cols = pl.ds(0, wide)
        Q[rows, cols] = Q[rows, cols] + XU[pl.ds(up(j * tile), tile), :]
        yu_copy(j).start()

    @pl.when(inner)
    def _():
        pass_on(0, 1)
        pass_on(1, 1)

    outs = [
        pltpu.make_async_copy(a, b, osem.at[k])
        for k, (a, b) in enumerate(((mixed_o, mixed_h), (tgrad_o, tgrad_h), (gup_o, gup_h), (gdown_o, gdown_h)))
    ]

    def total(a, out, own):
        part, from_near, from_far, _, _, recv = sets[a]
        to_near(a).wait_recv()
        remote(from_far, from_far, recv.at[1], recv.at[1], z_peer(z)).wait_recv()
        rows = pl.ds(up(z * T), T)
        out[...] = (
            own[rows, :].astype(jnp.float32)
            + part[rows, :].astype(jnp.float32)
            + from_near[...].astype(jnp.float32)
            + from_far[...].astype(jnp.float32)
        ).astype(jnp.bfloat16)
        outs[a].start()

    total(0, mixed_o, X)

    @pl.loop(0, tiles)
    def _(j):
        yd_copy(tiles + j).wait_recv()
        xd_copy(j).wait_recv()
        rows = pl.ds(up(x * H + j * tile), tile)
        piece = pl.ds(up(j * tile), tile)
        gdown_o[piece, :] = (
            Q[rows, pl.ds(up(wide + y * sl), sl)].astype(jnp.float32)
            + YD[pl.ds(up((tiles + j) * tile), tile), :].astype(jnp.float32)
            + XD[piece, :].astype(jnp.float32)
        ).astype(jnp.bfloat16)
        yu_copy(j).wait_recv()
        gup_o[piece, :] = Q[rows, pl.ds(up(y * sl), sl)] + YU[piece, :]

    outs[2].start()
    outs[3].start()
    total(1, tgrad_o, C)

    @pl.when(has_right)
    def _():
        own_block(0, tok_h, X, tok_s, tok_r, z_peer(right)).wait_send()
        own_block(0, cot_h, C, cot_s, cot_r, z_peer(right)).wait_send()

    @pl.when(has_left)
    def _():
        own_block(1, tok_h, X, tok_s, tok_r, z_peer(left)).wait_send()
        own_block(1, cot_h, C, cot_s, cot_r, z_peer(left)).wait_send()

    for k, src in ((1, near), (2, second), (3, last)):
        arrived_sends(k, src, X, tok_s, tok_r)
        arrived_sends(k, src, C, cot_s, cot_r)
    for k in range(1, s.n_z):
        gate_copy(k).wait_send()
    for item in wx_send:
        item.wait_send()
    for item in wy_send + wc_send:
        item.wait_send()
    for a in range(2):
        to_near(a).wait_send()
        for k in range(2):
            to_far(a, k).wait_send()

    @pl.loop(0, tiles)
    def _(j):
        xu_copy(j).wait_send()
        xd_copy(j).wait_send()
        yu_copy(j).wait_send()

    @pl.loop(0, steps)
    def _(j):
        yd_copy(j).wait_send()

    for item in outs:
        item.wait()


def finish_kernel(
    mixed_h, tgrad_h, gup_h, gdown_h, mixed_f, tgrad_f, gup_f, gdown_f, mixed_v, tgrad_v, gup_v, gdown_v, turned, into, out
):
    copies = []
    for k, (a, b) in enumerate(((gup_h, gup_v), (mixed_h, mixed_v), (tgrad_h, tgrad_v), (gdown_h, gdown_v))):
        copies.append(pltpu.make_async_copy(a, b, into.at[k]))
        copies[-1].start()
    back = [
        pltpu.make_async_copy(a, b, out.at[k])
        for k, (a, b) in enumerate(((turned, gup_f), (mixed_v, mixed_f), (tgrad_v, tgrad_f), (gdown_v, gdown_f)))
    ]
    copies[0].wait()
    for i in range(gup_v.shape[0]):
        turned[i] = gup_v[i].T
    for k in range(1, 4):
        copies[k].wait()
        back[k].start()
    back[0].start()
    for item in back:
        item.wait()


def per_device(tokens, routes, gates, cotangent, w_up, w_down):
    s = Sizes(lax.axis_size("expert"), lax.axis_size("dp"), tokens, routes, w_up)
    bf = jnp.bfloat16
    dma = pltpu.SemaphoreType.DMA
    wide = s.n_y * s.slice
    n_w = 4 * s.share
    steps = s.n_x * s.tiles
    block = (s.rows, s.width)
    scratch = [
        pltpu.VMEM((s.column, s.width), bf),
        pltpu.VMEM((s.column, s.width), bf),
        pltpu.VMEM((s.column, s.lanes), bf),
        pltpu.VMEM((s.width, s.units), bf),
        pltpu.VMEM((s.units, s.width), bf),
        pltpu.VMEM((s.column, s.units), bf),
        pltpu.VMEM((s.column, s.units), bf),
        pltpu.VMEM((s.rows, s.units), jnp.float32),
        pltpu.VMEM((s.column, s.width), bf),
        pltpu.VMEM((s.column, s.width), bf),
        pltpu.VMEM(block, bf), pltpu.VMEM(block, bf), pltpu.VMEM((2,) + block, bf),
        pltpu.VMEM(block, bf), pltpu.VMEM(block, bf), pltpu.VMEM((2,) + block, bf),
        pltpu.VMEM((s.units, 2 * wide), bf),
        pltpu.VMEM((2, s.tile, 2 * wide), bf),
        pltpu.VMEM((s.units, 2 * wide), bf),
        pltpu.VMEM((s.half, wide), bf),
        pltpu.VMEM((s.units, s.slice), bf),
        pltpu.VMEM((s.half, s.slice), bf),
        pltpu.VMEM((s.half, s.slice), bf),
        pltpu.VMEM(block, bf), pltpu.VMEM(block, bf),
        pltpu.VMEM((s.half, s.slice), bf), pltpu.VMEM((s.half, s.slice), bf),
        pltpu.VMEM((s.top, s.rows), jnp.int32), pltpu.VMEM((s.top, s.rows), jnp.float32),
        dma((5 + s.local,)), dma((4,)),
        dma((5,)), dma((s.n_z,)), dma((5,)), dma((s.n_z,)), dma((s.n_z,)), dma((s.n_z,)),
        dma((n_w,)), dma((n_w,)), dma((n_w,)), dma((n_w,)), dma((2 * n_w,)), dma((2 * n_w,)),
        dma((3,)), dma((4,)), dma((3,)), dma((4,)),
        dma((2 * steps,)), dma((2 * steps,)),
        dma((s.tiles,)), dma((s.tiles,)), dma((steps,)), dma((steps,)),
        dma((s.tiles,)), dma((s.tiles,)), dma((s.tiles,)), dma((s.tiles,)),
    ]
    any_space = pl.BlockSpec(memory_space=pl.ANY)
    parts = pl.pallas_call(
        functools.partial(step_kernel, s),
        out_shape=(
            jax.ShapeDtypeStruct(tokens.shape, bf),
            jax.ShapeDtypeStruct(tokens.shape, bf),
            jax.ShapeDtypeStruct((s.half, s.slice), bf),
            jax.ShapeDtypeStruct((s.half, s.slice), bf),
        ),
        in_specs=[any_space] * 6,
        out_specs=(any_space,) * 4,
        scratch_shapes=scratch,
        compiler_params=pltpu.CompilerParams(
            collective_id=0, has_side_effects=True, vmem_limit_bytes=67043328
        ),
        name="moe_step",
    )(tokens, routes.T, gates.T, cotangent, w_up, w_down.reshape(s.half, s.width))
    shapes = (
        tokens.shape,
        tokens.shape,
        (s.local, s.slice, s.hidden),
        (s.local, s.hidden, s.slice),
    )
    turned = (s.local, s.hidden, s.slice)
    mixed, token_grad, grad_up, grad_down = parts
    return pl.pallas_call(
        finish_kernel,
        out_shape=tuple(jax.ShapeDtypeStruct(shape, bf) for shape in shapes),
        in_specs=[any_space] * 4,
        out_specs=(any_space,) * 4,
        scratch_shapes=[
            pltpu.VMEM(tokens.shape, bf),
            pltpu.VMEM(tokens.shape, bf),
            pltpu.VMEM(turned, bf),
            pltpu.VMEM(turned, bf),
            pltpu.VMEM(shapes[2], bf),
            dma((4,)),
            dma((4,)),
        ],
        name="finish",
    )(mixed, token_grad, grad_up.reshape(turned), grad_down.reshape(turned))


def per_device_wide(tokens, routes, gates, cotangent, w_up, w_down):
    n_expert = lax.axis_size("expert")
    local_experts, model_width, hidden_width = w_up.shape
    experts_all = local_experts * n_expert
    tok_rows = tokens.shape[0]
    top_k = routes.shape[1]
    capacity = tok_rows * top_k // experts_all
    rows_all = n_expert * tok_rows
    units = local_experts * hidden_width

    gate_full = kept_gates(routes, gates, experts_all, capacity)
    gate_hi = gate_full.astype(jnp.bfloat16)
    gate_lo = (gate_full - gate_hi.astype(jnp.float32)).astype(jnp.bfloat16)
    gate_pair = jnp.concatenate([gate_hi, gate_lo], axis=1)

    all_tokens = lax.all_gather(tokens, "expert", axis=0, tiled=True)
    all_cot = lax.all_gather(
        jnp.concatenate([cotangent, gate_pair], axis=1), "expert", axis=0, tiled=True
    )
    first = lax.axis_index("expert") * local_experts
    all_gates = lax.dynamic_slice_in_dim(
        all_cot, model_width + first, local_experts, axis=1
    ).astype(jnp.float32) + lax.dynamic_slice_in_dim(
        all_cot, model_width + experts_all + first, local_experts, axis=1
    ).astype(jnp.float32)
    all_cot = all_cot[:, :model_width]
    gate_units = all_gates[:, :, None]

    pre_act = jnp.einsum("td,edf->tef", all_tokens, w_up, preferred_element_type=jnp.float32)
    value, slope = gelu_and_slope(pre_act)
    weighted = (value * gate_units).astype(jnp.bfloat16)
    mixed_part = jnp.einsum(
        "tef,efd->td", weighted, w_down, preferred_element_type=jnp.float32
    ).astype(jnp.bfloat16)
    mixed_sum = lax.psum_scatter(mixed_part, "expert", scatter_dimension=0, tiled=True)

    grad_hidden = jnp.einsum("td,efd->tef", all_cot, w_down, preferred_element_type=jnp.float32)
    grad_pre = (grad_hidden * slope * gate_units).astype(jnp.bfloat16)
    grad_part = jnp.einsum(
        "tef,edf->td", grad_pre, w_up, preferred_element_type=jnp.float32
    ).astype(jnp.bfloat16)
    grad_sum = lax.psum_scatter(grad_part, "expert", scatter_dimension=0, tiled=True)

    part_up = jnp.einsum(
        "td,tef->edf", all_tokens, grad_pre, preferred_element_type=jnp.float32
    ).astype(jnp.bfloat16)
    part_down = jnp.einsum(
        "tef,td->efd", weighted, all_cot, preferred_element_type=jnp.float32
    ).astype(jnp.bfloat16)
    up_sum = lax.psum_scatter(part_up, "dp", scatter_dimension=1, tiled=True)
    down_sum = lax.psum_scatter(part_down, "dp", scatter_dimension=2, tiled=True)

    mixed = (tokens.astype(jnp.float32) + mixed_sum.astype(jnp.float32)).astype(jnp.bfloat16)
    token_grad = (cotangent.astype(jnp.float32) + grad_sum.astype(jnp.float32)).astype(
        jnp.bfloat16
    )
    return (mixed, token_grad, up_sum, down_sum)


def solution(mesh):
    n_expert, n_dp = mesh.shape["expert"], mesh.shape["dp"]
    small = n_expert == 8 and n_dp == 4
    return jax.shard_map(
        per_device if small else per_device_wide,
        mesh=mesh,
        in_specs=(
            P(("expert", "dp"), None),
            P(("expert", "dp"), None),
            P(("expert", "dp"), None),
            P(("expert", "dp"), None),
            P("expert", None, None),
            P("expert", None, None),
        ),
        out_specs=(
            P(("expert", "dp"), None),
            P(("expert", "dp"), None),
            P("expert", "dp", None),
            P("expert", None, "dp"),
        ),
        check_vma=False,
    )
```

```python
import functools

import jax
import jax.numpy as jnp
from jax import lax
from jax.experimental import pallas as pl
from jax.experimental.pallas import tpu as pltpu
from jax.sharding import PartitionSpec as P

gelu_coef = 0.7978845608028654
cubic_coef = 0.044715
MESH = pl.DeviceIdType.MESH
CORES = 2


def gelu_and_slope(pre_act):
    square = pre_act * pre_act
    tanh_part = jnp.tanh(gelu_coef * pre_act * (1.0 + cubic_coef * square))
    value = 0.5 * pre_act * (1.0 + tanh_part)
    slope = 0.5 * (1.0 + tanh_part) + 0.5 * pre_act * (1.0 - tanh_part * tanh_part) * gelu_coef * (
        1.0 + 3.0 * cubic_coef * square
    )
    return value, slope


def kept_gates(routes, gates, experts_all, capacity):
    tok_rows = routes.shape[0]
    hits = routes[:, :, None] == jnp.arange(experts_all, dtype=jnp.int32)[None, None, :]
    named = jnp.any(hits, axis=1)
    gate_of = jnp.sum(jnp.where(hits, gates[:, :, None], jnp.float32(0.0)), axis=1)
    earlier = jnp.tril(jnp.ones((tok_rows, tok_rows), jnp.bfloat16), -1)
    rank = jnp.dot(earlier, named.astype(jnp.bfloat16), preferred_element_type=jnp.float32)
    return jnp.where(named & (rank < capacity), gate_of, jnp.float32(0.0))


def dot_nn(a, b):
    return lax.dot_general(a, b, (((1,), (0,)), ((), ())), preferred_element_type=jnp.float32)


def dot_nt(a, b):
    return lax.dot_general(a, b, (((1,), (1,)), ((), ())), preferred_element_type=jnp.float32)


class Sizes:
    def __init__(self, n_expert, n_dp, tokens, routes, w_up):
        self.n_y = n_dp // CORES
        self.n_x = n_dp // CORES
        self.n_z = n_expert // self.n_x
        self.local, self.width, self.hidden = w_up.shape
        self.rows = tokens.shape[0]
        self.top = routes.shape[1]
        self.experts = self.local * n_expert
        self.capacity = self.rows * self.top // self.experts
        self.half = self.local * self.hidden
        self.units = self.half * self.n_x
        self.column = self.rows * self.n_z
        self.slice = self.width // n_dp
        self.lanes = 2 * self.experts
        self.tile = 2 * self.hidden
        self.tiles = self.half // self.tile
        self.share = self.local // n_dp


def step_kernel(
    s,
    tok_h, routes_h, gates_h, cot_h, up_h, down_h,
    mixed_h, tgrad_h, gup_h, gdown_h,
    X, C, G, WU, WD, HT, GP, SL, MS, TS, MN, MP, MR, TN, TP, TR, Q, SB, CR, XU, YD, YU, XD,
    mixed_o, tgrad_o, gup_o, gdown_o, routes_v, gates_v,
    lsem, osem, tok_s, tok_r, cot_s, cot_r, gate_s, gate_r, wx_s, wx_r, wy_s, wy_r, wc_s, wc_r,
    m_s, m_r, g_s, g_r, core_s, core_r, xu_s, xu_r, yd_s, yd_r, xd_s, xd_r, yu_s, yu_r,
):
    e = lax.axis_index("expert")
    p = lax.axis_index("dp")
    z, x = e // s.n_x, e % s.n_x
    y, c = p // CORES, p % CORES
    T, H, F, D = s.rows, s.half, s.hidden, s.width
    tile, tiles, sl = s.tile, s.tiles, s.slice
    steps = s.n_x * tiles
    wide = s.n_y * sl

    def at(z_, x_, y_, c_):
        return (z_ * s.n_x + x_, y_ * CORES + c_)

    x_peer, y_peer, c_peer = at(z, 1 - x, y, c), at(z, x, 1 - y, c), at(z, x, y, 1 - c)

    def z_peer(zz):
        return at(zz, x, y, c)

    def remote(src, dst, send, recv, device):
        return pltpu.make_async_remote_copy(
            src_ref=src, dst_ref=dst, send_sem=send, recv_sem=recv, device_id=device, device_id_type=MESH
        )

    def up(n):
        return n if isinstance(n, int) else pl.multiple_of(n, 128)

    def block(ref, zz):
        return ref.at[pl.ds(up(zz * T), T)]

    own_up = [
        pltpu.make_async_copy(up_h.at[i], WU.at[:, pl.ds(up(x * H + i * F), F)], lsem.at[2 + i])
        for i in range(s.local)
    ]
    own_down = pltpu.make_async_copy(down_h, WD.at[pl.ds(up(x * H), H)], lsem.at[2 + s.local])
    own_tok = pltpu.make_async_copy(tok_h, block(X, z), lsem.at[0])
    own_cot = pltpu.make_async_copy(cot_h, block(C, z), lsem.at[1])
    own_routes = pltpu.make_async_copy(routes_h, routes_v, lsem.at[3 + s.local])
    own_gates = pltpu.make_async_copy(gates_h, gates_v, lsem.at[4 + s.local])

    barrier = pltpu.get_barrier_semaphore()
    peers = [z_peer((z + k) % s.n_z) for k in range(1, s.n_z)] + [x_peer, y_peer, c_peer]
    for peer in peers:
        pl.semaphore_signal(barrier, inc=1, device_id=peer, device_id_type=MESH)
    own_routes.start()
    own_gates.start()
    own_tok.start()
    own_cot.start()
    for item in own_up:
        item.start()
    own_down.start()
    pl.semaphore_wait(barrier, len(peers))

    has_right, has_left = z < s.n_z - 1, z > 0
    right, left = jnp.minimum(z + 1, s.n_z - 1), jnp.maximum(z - 1, 0)

    def own_block(which, src, ref, send, recv, device):
        return remote(src, block(ref, z), send.at[which], recv.at[z], device)

    first_x = (y * CORES + c) * s.share

    def weight_at(u, x_, base):
        i, half = base + u // 4, u % 2
        if u % 4 < 2:
            return WU.at[pl.ds(half * (D // 2), D // 2), pl.ds(up(x_ * H + i * F), F)]
        return WD.at[pl.ds(pl.multiple_of(x_ * H + i * F + half * (F // 2), F // 2), F // 2)]

    def weight_from(u):
        i, half = first_x + u // 4, u % 2
        if u % 4 < 2:
            return up_h.at[i, pl.ds(half * (D // 2), D // 2)]
        return down_h.at[pl.ds(pl.multiple_of(i * F + half * (F // 2), F // 2), F // 2)]

    n_w = 4 * s.share
    base_y = ((1 - y) * CORES + c) * s.share
    wx_send = [
        remote(weight_from(u), weight_at(u, x, first_x), wx_s.at[u], wx_r.at[u], x_peer) for u in range(n_w)
    ]
    wx_in = [
        remote(weight_from(u), weight_at(u, 1 - x, first_x), wx_s.at[u], wx_r.at[u], x_peer)
        for u in range(n_w)
    ]
    wy_send = [
        remote(weight_at(u, 1 - x, first_x), weight_at(u, 1 - x, first_x), wy_s.at[u], wy_r.at[u], y_peer)
        for u in range(n_w)
    ]
    wy_in = [
        remote(weight_at(u, 1 - x, base_y), weight_at(u, 1 - x, base_y), wy_s.at[u], wy_r.at[u], y_peer)
        for u in range(n_w)
    ]
    other_x = (y * CORES + 1 - c) * s.share
    other_y = ((1 - y) * CORES + 1 - c) * s.share
    wc_send = [
        remote(weight_at(u, 1 - x, b), weight_at(u, 1 - x, b), wc_s.at[k * n_w + u], wc_r.at[k * n_w + u], c_peer)
        for k, b in enumerate((first_x, base_y))
        for u in range(n_w)
    ]
    wc_in = [
        remote(weight_at(u, 1 - x, b), weight_at(u, 1 - x, b), wc_s.at[k * n_w + u], wc_r.at[k * n_w + u], c_peer)
        for k, b in enumerate((other_x, other_y))
        for u in range(n_w)
    ]

    @pl.when(has_right)
    def _():
        own_block(0, tok_h, X, tok_s, tok_r, z_peer(right)).start()
        own_block(0, cot_h, C, cot_s, cot_r, z_peer(right)).start()

    @pl.when(has_left)
    def _():
        own_block(1, tok_h, X, tok_s, tok_r, z_peer(left)).start()
        own_block(1, cot_h, C, cot_s, cot_r, z_peer(left)).start()

    for item in wx_send:
        item.start()

    own_routes.wait()
    own_gates.wait()
    E = s.experts
    line = lax.broadcasted_iota(jnp.int32, (s.lanes, T), 0)
    expert = jnp.where(line >= E, line - E, line)
    gate_of = jnp.zeros((s.lanes, T), jnp.float32)
    count = jnp.zeros((s.lanes, T), jnp.float32)
    for k in range(s.top):
        hit = routes_v[k : k + 1, :] == expert
        gate_of = gate_of + jnp.where(hit, gates_v[k : k + 1, :], 0.0)
        count = count + jnp.where(hit, 1.0, 0.0)
    tr = lax.broadcasted_iota(jnp.int32, (T, T), 0)
    tc = lax.broadcasted_iota(jnp.int32, (T, T), 1)
    earlier = jnp.where(tr < tc, 1.0, 0.0).astype(jnp.bfloat16)
    rank = dot_nn(count.astype(jnp.bfloat16), earlier)
    kept = jnp.where((count > 0.5) & (rank < s.capacity), gate_of, 0.0)
    high = kept.astype(jnp.bfloat16).astype(jnp.float32)
    G[pl.ds(up(z * T), T), :] = jnp.where(line >= E, kept - high, high).T.astype(jnp.bfloat16)

    def gate_copy(k):
        peer = (z + k) % s.n_z
        return remote(block(G, z), block(G, z), gate_s.at[k], gate_r.at[z], z_peer(peer))

    def gate_in(zz):
        remote(block(G, zz), block(G, zz), gate_s.at[0], gate_r.at[zz], z_peer(z)).wait_recv()

    near = z + 1 - 2 * (z % 2)
    second = jnp.where(z < s.n_z // 2, s.n_z // 2, s.n_z // 2 - 1)
    last = jnp.where(z < s.n_z // 2, s.n_z - 1, 0)
    inner = has_right & has_left

    def arrive(k, src, ref, send, recv):
        remote(block(ref, src), block(ref, src), send.at[1 + k], recv.at[src], z_peer(z)).wait_recv()
        onward = jnp.where(src < z, z + 1, z - 1)
        ok = (onward >= 0) & (onward < s.n_z)
        goal = jnp.clip(onward, 0, s.n_z - 1)

        @pl.when(ok)
        def _():
            remote(block(ref, src), block(ref, src), send.at[1 + k], recv.at[src], z_peer(goal)).start()

    def arrived_sends(k, src, ref, send, recv):
        onward = jnp.where(src < z, z + 1, z - 1)
        ok = (onward >= 0) & (onward < s.n_z)

        @pl.when(ok)
        def _():
            remote(block(ref, src), block(ref, src), send.at[1 + k], recv.at[src], z_peer(z)).wait_send()

    def weight_x(u):
        wx_in[u].wait_recv()
        wy_send[u].start()
        wc_send[u].start()

    def weight_y(u):
        wy_in[u].wait_recv()
        wc_send[n_w + u].start()

    def gate_tile(rows, t):
        first = z * s.n_x * s.local + t * (tile // F)
        ri = lax.broadcasted_iota(jnp.int32, (s.lanes, tile), 0)
        ci = lax.broadcasted_iota(jnp.int32, (s.lanes, tile), 1)
        goal = first + jnp.where(ci >= F, 1, 0)
        pick = jnp.where((ri == goal) | (ri == goal + E), 1.0, 0.0).astype(jnp.bfloat16)
        return dot_nn(G[rows, :], pick)

    def units(rows, tile0):
        @pl.loop(0, tiles)
        def _(n):
            cols = pl.ds(up((tile0 + n) * tile), tile)
            gate = gate_tile(rows, tile0 + n)
            value, slope = gelu_and_slope(dot_nn(X[rows, :], WU[:, cols]))
            HT[rows, cols] = (value * gate).astype(jnp.bfloat16)
            grad_hidden = dot_nt(C[rows, :], WD[cols, :])
            GP[rows, cols] = (grad_hidden * (slope * gate)).astype(jnp.bfloat16)

    def forward_units(rows):
        @pl.loop(0, steps)
        def _(n):
            cols = pl.ds(up(n * tile), tile)
            gate = gate_tile(rows, n)
            value, slope = gelu_and_slope(dot_nn(X[rows, :], WU[:, cols]))
            HT[rows, cols] = (value * gate).astype(jnp.bfloat16)
            SL[:, cols] = slope * gate

    def backward_tile(rows, u0):
        cols = pl.ds(u0, tile)
        GP[rows, cols] = (dot_nt(C[rows, :], WD[cols, :]) * SL[:, cols]).astype(jnp.bfloat16)

    def mix_tile(rows, n):
        cols = pl.ds(up(n * tile), tile)
        MS[rows, cols] = dot_nn(HT[rows, :], WD[:, cols]).astype(jnp.bfloat16)

    def grad_tile(rows, n):
        cols = pl.ds(up(n * tile), tile)
        TS[rows, cols] = dot_nt(GP[rows, :], WU[cols, :]).astype(jnp.bfloat16)

    def mix_side(rows, side, add):
        inner_cols = pl.ds(up(side * H), H)

        @pl.loop(0, steps)
        def _(n):
            cols = pl.ds(up(n * tile), tile)
            value = dot_nn(HT[rows, inner_cols], WD[inner_cols, cols])
            if add:
                value = value + MS[rows, cols].astype(jnp.float32)
            MS[rows, cols] = value.astype(jnp.bfloat16)

    def grad_side(rows, side):
        inner_cols = pl.ds(up(side * H), H)

        @pl.loop(0, steps)
        def _(n):
            cols = pl.ds(up(n * tile), tile)
            TS[rows, cols] = dot_nt(GP[rows, inner_cols], WU[cols, inner_cols]).astype(jnp.bfloat16)

    def grad_rest_tile(rows, side, n):
        inner_cols = pl.ds(up(side * H), H)
        cols = pl.ds(up(n * tile), tile)
        value = dot_nt(GP[rows, inner_cols], WU[cols, inner_cols]) + TS[rows, cols].astype(jnp.float32)
        TS[rows, cols] = value.astype(jnp.bfloat16)

    sets = ((MS, MN, MP, MR, m_s, m_r), (TS, TN, TP, TR, g_s, g_r))

    def to_near(a):
        part, into, _, _, send, recv = sets[a]
        return remote(block(part, near), into, send.at[0], recv.at[0], z_peer(near))

    def to_relay(a, k):
        part, _, _, into, send, recv = sets[a]
        return remote(block(part, (second, last)[k]), into.at[k], send.at[1 + k], recv.at[2 + k], z_peer(near))

    def to_far(a, k):
        part, _, into, _, send, recv = sets[a]
        goal = (second, last)[k]
        return remote(block(part, goal), into, send.at[1 + k], recv.at[1], z_peer(goal))

    def pass_on(a, k):
        part, _, _, into, _, _ = sets[a]
        to_relay(a, k).wait_recv()
        rows = pl.ds(up((second, last)[k] * T), T)
        part[rows, :] = part[rows, :] + into[k]
        to_far(a, k).start()

    own_tok.wait()
    own_cot.wait()
    for k in range(1, s.n_z):
        gate_copy(k).start()
    for item in own_up:
        item.wait()
    own_down.wait()

    low = z < s.n_z // 2
    pair = pl.ds(up(jnp.where(low, 0, 2 * T)), 2 * T)
    single = pl.ds(up(second * T), T)
    most = pl.ds(up(jnp.where(low, 0, T)), (s.n_z - 1) * T)
    rest = pl.ds(up(last * T), T)

    weight_x(0)
    weight_x(1)
    arrive(1, near, X, tok_s, tok_r)
    weight_y(0)
    weight_x(2)
    weight_y(1)
    weight_x(3)
    arrive(1, near, C, cot_s, cot_r)
    weight_y(2)

    @pl.when(inner)
    def _():
        arrive(2, second, X, tok_s, tok_r)

    gate_in(near)
    units(pair, x * tiles)
    weight_x(4)
    weight_y(3)
    mix_side(pair, x, False)

    @pl.when(inner)
    def _():
        arrive(2, second, C, cot_s, cot_r)

    grad_side(pair, x)
    weight_x(5)
    weight_y(4)

    @pl.when(jnp.logical_not(inner))
    def _():
        arrive(2, second, X, tok_s, tok_r)

    weight_x(6)
    weight_y(5)

    @pl.when(inner)
    def _():
        arrive(3, last, X, tok_s, tok_r)

    weight_x(7)
    weight_y(6)

    @pl.when(jnp.logical_not(inner))
    def _():
        arrive(2, second, C, cot_s, cot_r)

    gate_in(second)
    gate_in(last)
    units(single, x * tiles)
    mix_side(single, x, False)
    grad_side(single, x)

    @pl.when(inner)
    def _():
        arrive(3, last, C, cot_s, cot_r)

    weight_y(7)
    for item in wc_in:
        item.wait_recv()
    units(most, (1 - x) * tiles)
    mix_side(most, 1 - x, True)

    @pl.when(jnp.logical_not(inner))
    def _():
        to_relay(0, 0).start()

    to_near(0).start()

    @pl.when(jnp.logical_not(inner))
    def _():
        arrive(3, last, X, tok_s, tok_r)

    forward_units(rest)

    @pl.when(jnp.logical_not(inner))
    def _():
        arrive(3, last, C, cot_s, cot_r)

    def unit_rows(i):
        side = jnp.where(i < tiles, 1 - x, x)
        return up(side * H + (i % tiles) * tile)

    def core_copy(i, arr):
        rows, cols = pl.ds(unit_rows(i), tile), pl.ds(arr * wide, wide)
        return remote(
            SB.at[i % 2, :, cols], CR.at[rows, cols],
            core_s.at[arr * steps + i], core_r.at[arr * steps + i], c_peer,
        )

    def xu_copy(i):
        return remote(
            Q.at[pl.ds(unit_rows(i), tile), pl.ds(0, wide)], XU.at[pl.ds(up(i * tile), tile)],
            xu_s.at[i], xu_r.at[i], x_peer,
        )

    def yd_copy(i):
        return remote(
            Q.at[pl.ds(unit_rows(i), tile), pl.ds(up(wide + (1 - y) * sl), sl)],
            YD.at[pl.ds(up(i * tile), tile)], yd_s.at[i], yd_r.at[i], y_peer,
        )

    def xd_copy(j):
        return remote(
            Q.at[pl.ds(up((1 - x) * H + j * tile), tile), pl.ds(up(wide + y * sl), sl)],
            XD.at[pl.ds(up(j * tile), tile)], xd_s.at[j], xd_r.at[j], x_peer,
        )

    def yu_copy(j):
        return remote(
            Q.at[pl.ds(up(x * H + j * tile), tile), pl.ds(up((1 - y) * sl), sl)],
            YU.at[pl.ds(up(j * tile), tile)], yu_s.at[j], yu_r.at[j], y_peer,
        )

    def give_part(i, arr, left_ref, right_ref):
        @pl.when(i >= 2)
        def _():
            core_copy(jnp.maximum(i - 2, 0), arr).wait_send()

        left_t = left_ref[:, pl.ds(unit_rows(i), tile)].T
        for yy in range(s.n_y):
            to = pl.ds((arr * s.n_y + yy) * sl, sl)
            theirs = pl.ds(up((yy * CORES + 1 - c) * sl), sl)
            SB[i % 2, :, to] = dot_nn(left_t, right_ref[:, theirs]).astype(jnp.bfloat16)
        core_copy(i, arr).start()
        return left_t

    def keep_part(i, arr, left_t, right_ref):
        rows = pl.ds(unit_rows(i), tile)
        for yy in range(s.n_y):
            to = pl.ds((arr * s.n_y + yy) * sl, sl)
            mine = pl.ds(up((yy * CORES + c) * sl), sl)
            Q[rows, to] = dot_nn(left_t, right_ref[:, mine]).astype(jnp.bfloat16)

    def join(i, arr):
        core_copy(i, arr).wait_recv()
        rows, cols = pl.ds(unit_rows(i), tile), pl.ds(arr * wide, wide)
        Q[rows, cols] = Q[rows, cols] + CR[rows, cols]

    @pl.loop(0, steps)
    def _(i):
        hid_t = give_part(i, 1, HT, C)
        backward_tile(rest, unit_rows(i))
        grad_t = give_part(i, 0, GP, X)
        keep_part(i, 1, hid_t, C)
        join(i, 1)
        yd_copy(i).start()
        keep_part(i, 0, grad_t, X)
        join(i, 0)

        @pl.when(i < tiles)
        def _():
            xu_copy(i).start()
            for k in range(s.n_x):
                grad_rest_tile(most, 1 - x, s.n_x * i + k)

        @pl.when(i >= tiles)
        def _():
            for k in range(s.n_x):
                mix_tile(rest, s.n_x * (i - tiles) + k)

        @pl.when((i == tiles - 1) & inner)
        def _():
            to_near(1).start()
            pass_on(0, 0)

        @pl.when((i == tiles - 1) & jnp.logical_not(inner))
        def _():
            to_relay(1, 0).start()

    for k in range(2):
        core_copy(steps - 2 + k, 0).wait_send()
        core_copy(steps - 2 + k, 1).wait_send()

    @pl.when(jnp.logical_not(inner))
    def _():
        to_relay(0, 1).start()

    @pl.loop(0, steps)
    def _(n):
        grad_tile(rest, n)

    @pl.when(jnp.logical_not(inner))
    def _():
        to_relay(1, 1).start()
        to_near(1).start()

    @pl.when(inner)
    def _():
        pass_on(1, 0)

    @pl.loop(0, tiles)
    def _(j):
        yd_copy(j).wait_recv()
        rows = pl.ds(up((1 - x) * H + j * tile), tile)
        cols = pl.ds(up(wide + y * sl), sl)
        Q[rows, cols] = Q[rows, cols] + YD[pl.ds(up(j * tile), tile), :]
        xd_copy(j).start()

    @pl.loop(0, tiles)
    def _(j):
        xu_copy(j).wait_recv()
        rows = pl.ds(up(x * H + j * tile), tile)
        cols = pl.ds(0, wide)
        Q[rows, cols] = Q[rows, cols] + XU[pl.ds(up(j * tile), tile), :]
        yu_copy(j).start()

    @pl.when(inner)
    def _():
        pass_on(0, 1)
        pass_on(1, 1)

    outs = [
        pltpu.make_async_copy(a, b, osem.at[k])
        for k, (a, b) in enumerate(((mixed_o, mixed_h), (tgrad_o, tgrad_h)))
    ]

    def weight_out(j, k):
        piece = pl.ds(up(j * tile), tile)
        a, b = ((gup_o, gup_h), (gdown_o, gdown_h))[k]
        return pltpu.make_async_copy(a.at[piece], b.at[piece], osem.at[2 + 2 * j + k])

    def total(a, out, own):
        part, from_near, from_far, _, _, recv = sets[a]
        to_near(a).wait_recv()
        remote(from_far, from_far, recv.at[1], recv.at[1], z_peer(z)).wait_recv()
        rows = pl.ds(up(z * T), T)
        out[...] = (
            own[rows, :].astype(jnp.float32)
            + part[rows, :].astype(jnp.float32)
            + from_near[...].astype(jnp.float32)
            + from_far[...].astype(jnp.float32)
        ).astype(jnp.bfloat16)
        outs[a].start()

    total(0, mixed_o, X)

    def last_sum(j):
        yd_copy(tiles + j).wait_recv()
        xd_copy(j).wait_recv()
        rows = pl.ds(up(x * H + j * tile), tile)
        piece = pl.ds(up(j * tile), tile)
        gdown_o[piece, :] = (
            Q[rows, pl.ds(up(wide + y * sl), sl)].astype(jnp.float32)
            + YD[pl.ds(up((tiles + j) * tile), tile), :].astype(jnp.float32)
            + XD[piece, :].astype(jnp.float32)
        ).astype(jnp.bfloat16)
        yu_copy(j).wait_recv()
        weight_out(j, 1).start()
        gup_o[piece, :] = Q[rows, pl.ds(up(y * sl), sl)] + YU[piece, :]
        weight_out(j, 0).start()

    @pl.loop(0, tiles - 1)
    def _(j):
        last_sum(j)

    total(1, tgrad_o, C)
    last_sum(tiles - 1)

    @pl.when(has_right)
    def _():
        own_block(0, tok_h, X, tok_s, tok_r, z_peer(right)).wait_send()
        own_block(0, cot_h, C, cot_s, cot_r, z_peer(right)).wait_send()

    @pl.when(has_left)
    def _():
        own_block(1, tok_h, X, tok_s, tok_r, z_peer(left)).wait_send()
        own_block(1, cot_h, C, cot_s, cot_r, z_peer(left)).wait_send()

    for k, src in ((1, near), (2, second), (3, last)):
        arrived_sends(k, src, X, tok_s, tok_r)
        arrived_sends(k, src, C, cot_s, cot_r)
    for k in range(1, s.n_z):
        gate_copy(k).wait_send()
    for item in wx_send:
        item.wait_send()
    for item in wy_send + wc_send:
        item.wait_send()
    for a in range(2):
        to_near(a).wait_send()
        for k in range(2):
            to_far(a, k).wait_send()

    @pl.loop(0, tiles)
    def _(j):
        xu_copy(j).wait_send()
        xd_copy(j).wait_send()
        yu_copy(j).wait_send()

    @pl.loop(0, steps)
    def _(j):
        yd_copy(j).wait_send()

    for item in outs:
        item.wait()

    @pl.loop(0, tiles)
    def _(j):
        weight_out(j, 0).wait()
        weight_out(j, 1).wait()


def finish_kernel(
    mixed_h, tgrad_h, gup_h, gdown_h, mixed_f, tgrad_f, gup_f, gdown_f, mixed_v, tgrad_v, gup_v, gdown_v, turned, into, out
):
    copies = []
    for k, (a, b) in enumerate(((gup_h, gup_v), (mixed_h, mixed_v), (tgrad_h, tgrad_v), (gdown_h, gdown_v))):
        copies.append(pltpu.make_async_copy(a, b, into.at[k]))
        copies[-1].start()
    back = [
        pltpu.make_async_copy(a, b, out.at[k])
        for k, (a, b) in enumerate(((turned, gup_f), (mixed_v, mixed_f), (tgrad_v, tgrad_f), (gdown_v, gdown_f)))
    ]
    copies[0].wait()
    for i in range(gup_v.shape[0]):
        turned[i] = gup_v[i].T
    for k in range(1, 4):
        copies[k].wait()
        back[k].start()
    back[0].start()
    for item in back:
        item.wait()


def per_device(tokens, routes, gates, cotangent, w_up, w_down):
    s = Sizes(lax.axis_size("expert"), lax.axis_size("dp"), tokens, routes, w_up)
    bf = jnp.bfloat16
    dma = pltpu.SemaphoreType.DMA
    wide = s.n_y * s.slice
    n_w = 4 * s.share
    steps = s.n_x * s.tiles
    block = (s.rows, s.width)
    scratch = [
        pltpu.VMEM((s.column, s.width), bf),
        pltpu.VMEM((s.column, s.width), bf),
        pltpu.VMEM((s.column, s.lanes), bf),
        pltpu.VMEM((s.width, s.units), bf),
        pltpu.VMEM((s.units, s.width), bf),
        pltpu.VMEM((s.column, s.units), bf),
        pltpu.VMEM((s.column, s.units), bf),
        pltpu.VMEM((s.rows, s.units), jnp.float32),
        pltpu.VMEM((s.column, s.width), bf),
        pltpu.VMEM((s.column, s.width), bf),
        pltpu.VMEM(block, bf), pltpu.VMEM(block, bf), pltpu.VMEM((2,) + block, bf),
        pltpu.VMEM(block, bf), pltpu.VMEM(block, bf), pltpu.VMEM((2,) + block, bf),
        pltpu.VMEM((s.units, 2 * wide), bf),
        pltpu.VMEM((2, s.tile, 2 * wide), bf),
        pltpu.VMEM((s.units, 2 * wide), bf),
        pltpu.VMEM((s.half, wide), bf),
        pltpu.VMEM((s.units, s.slice), bf),
        pltpu.VMEM((s.half, s.slice), bf),
        pltpu.VMEM((s.half, s.slice), bf),
        pltpu.VMEM(block, bf), pltpu.VMEM(block, bf),
        pltpu.VMEM((s.half, s.slice), bf), pltpu.VMEM((s.half, s.slice), bf),
        pltpu.VMEM((s.top, s.rows), jnp.int32), pltpu.VMEM((s.top, s.rows), jnp.float32),
        dma((5 + s.local,)), dma((2 + 2 * s.tiles,)),
        dma((5,)), dma((s.n_z,)), dma((5,)), dma((s.n_z,)), dma((s.n_z,)), dma((s.n_z,)),
        dma((n_w,)), dma((n_w,)), dma((n_w,)), dma((n_w,)), dma((2 * n_w,)), dma((2 * n_w,)),
        dma((3,)), dma((4,)), dma((3,)), dma((4,)),
        dma((2 * steps,)), dma((2 * steps,)),
        dma((s.tiles,)), dma((s.tiles,)), dma((steps,)), dma((steps,)),
        dma((s.tiles,)), dma((s.tiles,)), dma((s.tiles,)), dma((s.tiles,)),
    ]
    any_space = pl.BlockSpec(memory_space=pl.ANY)
    parts = pl.pallas_call(
        functools.partial(step_kernel, s),
        out_shape=(
            jax.ShapeDtypeStruct(tokens.shape, bf),
            jax.ShapeDtypeStruct(tokens.shape, bf),
            jax.ShapeDtypeStruct((s.half, s.slice), bf),
            jax.ShapeDtypeStruct((s.half, s.slice), bf),
        ),
        in_specs=[any_space] * 6,
        out_specs=(any_space,) * 4,
        scratch_shapes=scratch,
        compiler_params=pltpu.CompilerParams(
            collective_id=0, has_side_effects=True, vmem_limit_bytes=67043328
        ),
        name="moe_step",
    )(tokens, routes.T, gates.T, cotangent, w_up, w_down.reshape(s.half, s.width))
    shapes = (
        tokens.shape,
        tokens.shape,
        (s.local, s.slice, s.hidden),
        (s.local, s.hidden, s.slice),
    )
    turned = (s.local, s.hidden, s.slice)
    mixed, token_grad, grad_up, grad_down = parts
    return pl.pallas_call(
        finish_kernel,
        out_shape=tuple(jax.ShapeDtypeStruct(shape, bf) for shape in shapes),
        in_specs=[any_space] * 4,
        out_specs=(any_space,) * 4,
        scratch_shapes=[
            pltpu.VMEM(tokens.shape, bf),
            pltpu.VMEM(tokens.shape, bf),
            pltpu.VMEM(turned, bf),
            pltpu.VMEM(turned, bf),
            pltpu.VMEM(shapes[2], bf),
            dma((4,)),
            dma((4,)),
        ],
        name="finish",
    )(mixed, token_grad, grad_up.reshape(turned), grad_down.reshape(turned))


def per_device_wide(tokens, routes, gates, cotangent, w_up, w_down):
    n_expert = lax.axis_size("expert")
    local_experts, model_width, hidden_width = w_up.shape
    experts_all = local_experts * n_expert
    tok_rows = tokens.shape[0]
    top_k = routes.shape[1]
    capacity = tok_rows * top_k // experts_all
    rows_all = n_expert * tok_rows
    units = local_experts * hidden_width

    gate_full = kept_gates(routes, gates, experts_all, capacity)
    gate_hi = gate_full.astype(jnp.bfloat16)
    gate_lo = (gate_full - gate_hi.astype(jnp.float32)).astype(jnp.bfloat16)
    gate_pair = jnp.concatenate([gate_hi, gate_lo], axis=1)

    all_tokens = lax.all_gather(tokens, "expert", axis=0, tiled=True)
    all_cot = lax.all_gather(
        jnp.concatenate([cotangent, gate_pair], axis=1), "expert", axis=0, tiled=True
    )
    first = lax.axis_index("expert") * local_experts
    all_gates = lax.dynamic_slice_in_dim(
        all_cot, model_width + first, local_experts, axis=1
    ).astype(jnp.float32) + lax.dynamic_slice_in_dim(
        all_cot, model_width + experts_all + first, local_experts, axis=1
    ).astype(jnp.float32)
    all_cot = all_cot[:, :model_width]
    gate_units = all_gates[:, :, None]

    pre_act = jnp.einsum("td,edf->tef", all_tokens, w_up, preferred_element_type=jnp.float32)
    value, slope = gelu_and_slope(pre_act)
    weighted = (value * gate_units).astype(jnp.bfloat16)
    mixed_part = jnp.einsum(
        "tef,efd->td", weighted, w_down, preferred_element_type=jnp.float32
    ).astype(jnp.bfloat16)
    mixed_sum = lax.psum_scatter(mixed_part, "expert", scatter_dimension=0, tiled=True)

    grad_hidden = jnp.einsum("td,efd->tef", all_cot, w_down, preferred_element_type=jnp.float32)
    grad_pre = (grad_hidden * slope * gate_units).astype(jnp.bfloat16)
    grad_part = jnp.einsum(
        "tef,edf->td", grad_pre, w_up, preferred_element_type=jnp.float32
    ).astype(jnp.bfloat16)
    grad_sum = lax.psum_scatter(grad_part, "expert", scatter_dimension=0, tiled=True)

    part_up = jnp.einsum(
        "td,tef->edf", all_tokens, grad_pre, preferred_element_type=jnp.float32
    ).astype(jnp.bfloat16)
    part_down = jnp.einsum(
        "tef,td->efd", weighted, all_cot, preferred_element_type=jnp.float32
    ).astype(jnp.bfloat16)
    up_sum = lax.psum_scatter(part_up, "dp", scatter_dimension=1, tiled=True)
    down_sum = lax.psum_scatter(part_down, "dp", scatter_dimension=2, tiled=True)

    mixed = (tokens.astype(jnp.float32) + mixed_sum.astype(jnp.float32)).astype(jnp.bfloat16)
    token_grad = (cotangent.astype(jnp.float32) + grad_sum.astype(jnp.float32)).astype(
        jnp.bfloat16
    )
    return (mixed, token_grad, up_sum, down_sum)


def solution(mesh):
    n_expert, n_dp = mesh.shape["expert"], mesh.shape["dp"]
    small = n_expert == 8 and n_dp == 4
    return jax.shard_map(
        per_device if small else per_device_wide,
        mesh=mesh,
        in_specs=(
            P(("expert", "dp"), None),
            P(("expert", "dp"), None),
            P(("expert", "dp"), None),
            P(("expert", "dp"), None),
            P("expert", None, None),
            P("expert", None, None),
        ),
        out_specs=(
            P(("expert", "dp"), None),
            P(("expert", "dp"), None),
            P("expert", "dp", None),
            P("expert", None, "dp"),
        ),
        check_vma=False,
    )
```
